128 devices in a mesh: dp: 32 (over z, x, y_lo), tensor: 4 (over y_hi, core).
Axes of the slice: x: 4, y: 4 (y_hi: 2, y_lo: 2; y = y_hi * 2 + y_lo), z: 4, core: 2. Of those that a mesh axis runs over, the one named last changes fastest.
Arguments:
- acts: bfloat16 [16384, 4096], P(('dp', 'tensor')), may hold values from -6 to 6
- out_grad: bfloat16 [16384, 16384], P('dp', 'tensor'), may hold values from -0.09375 to 0.09375
- projector: bfloat16 [4096, 512], replicated, may hold values from -0.09375 to 0.09375
- weight: bfloat16 [4096, 16384], P('dp', 'tensor'), may hold values from -6 to 6
- first_moment: float32 [4, 4096, 512], P('tensor', 'dp'), may hold values from -4 to 4
- second_moment: float32 [4, 4096, 512], P('tensor', 'dp'), may hold values from 0.01 to 1
Outputs:
- new_weight: bfloat16 [4096, 16384], P('dp', 'tensor')
- new_first: float32 [4, 4096, 512], P('tensor', 'dp')
- new_second: float32 [4, 4096, 512], P('tensor', 'dp')
The draws below stay inside these ranges and needn't reach their ends.
All inputs are finite; a program needn't handle non-finite values.
Results may differ from the reference program's by a relative error of at most 0.015.
Values may be sent and summed in bfloat16 or wider, within the bound.
A program may use at most 128 MiB of HBM per device.

```python
import math
import jax
import jax.numpy as jnp
from jax import lax

WIDTH = 4096
HIDDEN_SIZE = 16384
RANK = 512
TOK_DEV = 512
TOKENS = 16384
N_DP = 32
N_TENSOR = 4


def with_spikes(array, own_key, source, target, parts, factor):
    owner, partner = [(jnp.arange(array.shape[axis_at]) // (array.shape[axis_at] // parts)).reshape([-1 if axis == axis_at else 1 for axis in range(array.ndim)]) for axis_at in (source, target)]
    chosen = jax.random.permutation(own_key, parts)[partner]
    strong = (owner == chosen) | (owner == (partner + parts // 2) % parts)
    return jnp.where(strong, factor * array, array)


def block_scale(own_key, shape, split, smallest, largest):
    gain = 1.0
    for dim, parts in split:
        steps = jax.random.uniform(jax.random.fold_in(jax.random.fold_in(own_key, 6), dim), (parts,), jnp.float32, smallest / len(split), largest / len(split))
        gain = gain * jnp.repeat(jnp.exp(steps), shape[dim] // parts).reshape((-1,) + (1,) * (len(shape) - 1 - dim))
    return gain


def centred(stream_key, dims, deviation, bound, shards=(), dtype=jnp.bfloat16):
    entries = deviation * jax.random.normal(stream_key, dims, jnp.float32)
    if shards:
        entries = entries * block_scale(stream_key, dims, shards, -0.22, 0.18)
    return jnp.clip(entries, -bound, bound).astype(dtype)


def noise_with(key, dims, deviation, most, pieces, heavy, held_as=jnp.bfloat16):
    array = deviation * jax.random.normal(key, dims, jnp.float32)
    if pieces:
        array = array * block_scale(key, dims, pieces, -0.22, 0.18)
    return jnp.clip(with_spikes(array, jax.random.fold_in(key, 3), *heavy), -most, most).astype(held_as)


def setup_inputs(seed: int = 0) -> dict:
    key_of = jax.random.split(jax.random.key(seed), 7)
    return {
        "acts": centred(key_of[0], (TOKENS, WIDTH), 1.0, 6.0, ((0, 128),)),
        "out_grad": noise_with(key_of[1], (TOKENS, HIDDEN_SIZE), TOKENS ** -0.5, 0.09375, ((0, 32), (1, 4)), (0, 1, 32, 2.75)),
        "projector": centred(key_of[2], (WIDTH, RANK), WIDTH ** -0.5, 0.09375),
        "weight": centred(key_of[3], (WIDTH, HIDDEN_SIZE), 1.0, 6.0, ((0, 32), (1, 4))),
        "first_moment": centred(key_of[4], (N_TENSOR, HIDDEN_SIZE // N_TENSOR, RANK), 0.3, 4.0, ((0, 4), (1, 32)), jnp.float32),
        "second_moment": jnp.clip(jnp.exp(math.log(1.0) - 4.6051702 * jax.random.uniform(key_of[5], (N_TENSOR, HIDDEN_SIZE // N_TENSOR, RANK), jnp.float32) ** block_scale(key_of[5], (N_TENSOR, HIDDEN_SIZE // N_TENSOR, RANK), ((0, 4), (1, 32)), -0.2, 0.2)), 0.01, 1.0),
    }


beta_first = 0.9
beta_second = 0.95
adam_step = 10
epsilon = 1e-08
step_rate = 0.5

def adam_moments(lowgrad, first_moment, second_moment):
    new_first = beta_first * first_moment + (1.0 - beta_first) * lowgrad
    new_second = beta_second * second_moment + (1.0 - beta_second) * lowgrad * lowgrad
    corrected_first = new_first / (1.0 - beta_first ** adam_step)
    corrected_second = new_second / (1.0 - beta_second ** adam_step)
    direction = (corrected_first / (jnp.sqrt(corrected_second) + epsilon)).astype(jnp.bfloat16)
    return (new_first, new_second, direction)

def reference(acts, out_grad, projector, weight, first_moment, second_moment):
    acts_groups = acts.reshape(N_DP, TOK_DEV, WIDTH)
    grad_groups = out_grad.reshape(N_DP, TOK_DEV, HIDDEN_SIZE)

    def add_group(total, pair):
        group_acts, group_grad = pair
        partial_grad = lax.dot_general(group_grad, group_acts, (((0,), (0,)), ((), ())), preferred_element_type=jnp.float32)
        rounded = lax.optimization_barrier(partial_grad.astype(jnp.bfloat16))
        return (total + rounded.astype(jnp.float32), None)
    total, unused = lax.scan(add_group, jnp.zeros((HIDDEN_SIZE, WIDTH), jnp.float32), (acts_groups, grad_groups))
    lowgrad = jnp.dot(total, projector.astype(jnp.float32), precision=lax.Precision.HIGHEST, preferred_element_type=jnp.float32)
    new_first, new_second, direction = adam_moments(lowgrad, first_moment.reshape(HIDDEN_SIZE, RANK), second_moment.reshape(HIDDEN_SIZE, RANK))
    update = lax.dot_general(projector, direction, (((1,), (1,)), ((), ())), preferred_element_type=jnp.float32)
    update = lax.optimization_barrier(update.astype(jnp.bfloat16))
    new_weight = (weight.astype(jnp.float32) - step_rate * update.astype(jnp.float32)).astype(jnp.bfloat16)
    shape = (N_TENSOR, HIDDEN_SIZE // N_TENSOR, RANK)
    return (new_weight, new_first.reshape(shape), new_second.reshape(shape))
```

```python
import jax
import jax.numpy as jnp
from jax import lax
from jax.sharding import PartitionSpec as P

beta_first = 0.9
beta_second = 0.95
adam_step = 10
epsilon = 1e-08
step_rate = 0.5


def adam_moments(lowgrad, first_moment, second_moment):
    new_first = beta_first * first_moment + (1.0 - beta_first) * lowgrad
    new_second = beta_second * second_moment + (1.0 - beta_second) * lowgrad * lowgrad
    corrected_first = new_first / (1.0 - beta_first**adam_step)
    corrected_second = new_second / (1.0 - beta_second**adam_step)
    direction = (corrected_first / (jnp.sqrt(corrected_second) + epsilon)).astype(jnp.bfloat16)
    return (new_first, new_second, direction)


def per_device(acts, out_grad, projector, weight, first_moment, second_moment):
    token_proj = jnp.dot(acts, projector, preferred_element_type=jnp.float32)
    peers = lax.axis_size("tensor")
    whole_proj = lax.all_to_all(
        jnp.tile(token_proj, (peers, 1)), "tensor", split_axis=0, concat_axis=0, tiled=True
    )
    proj_hi = whole_proj.astype(jnp.bfloat16)
    proj_lo = (whole_proj - proj_hi.astype(jnp.float32)).astype(jnp.bfloat16)
    dims = (((0,), (0,)), ((), ()))
    partial = lax.dot_general(
        out_grad, proj_hi, dims, preferred_element_type=jnp.float32
    ) + lax.dot_general(out_grad, proj_lo, dims, preferred_element_type=jnp.float32)
    owners = lax.axis_size("dp")
    blocks = lax.all_to_all(
        partial.astype(jnp.bfloat16).reshape(owners, -1, partial.shape[1]),
        "dp",
        split_axis=0,
        concat_axis=0,
        tiled=True,
    )
    lowgrad = jnp.sum(blocks.astype(jnp.float32), axis=0)
    new_first, new_second, direction = adam_moments(lowgrad, first_moment[0], second_moment[0])
    owned_update = lax.dot_general(
        projector, direction, (((1,), (1,)), ((), ())), preferred_element_type=jnp.float32
    ).astype(jnp.bfloat16)
    update = lax.all_to_all(owned_update, "dp", split_axis=0, concat_axis=1, tiled=True)
    new_weight = (weight.astype(jnp.float32) - step_rate * update.astype(jnp.float32)).astype(
        jnp.bfloat16
    )
    return (new_weight, new_first[None], new_second[None])


def solution(mesh):
    return jax.shard_map(
        per_device,
        mesh=mesh,
        in_specs=(
            P(("dp", "tensor"), None),
            P("dp", "tensor"),
            P(),
            P("dp", "tensor"),
            P("tensor", "dp", None),
            P("tensor", "dp", None),
        ),
        out_specs=(P("dp", "tensor"), P("tensor", "dp", None), P("tensor", "dp", None)),
        check_vma=False,
    )
```

```python
import functools

import jax
import jax.numpy as jnp
from jax import lax
from jax.experimental import pallas as pl
from jax.experimental.pallas import tpu as pltpu
from jax.sharding import PartitionSpec as P

beta_first = 0.9
beta_second = 0.95
adam_step = 10
epsilon = 1e-08
step_rate = 0.5

MESH_ID = pl.DeviceIdType.MESH


def adam_moments(lowgrad, first_moment, second_moment):
    new_first = beta_first * first_moment + (1.0 - beta_first) * lowgrad
    new_second = beta_second * second_moment + (1.0 - beta_second) * lowgrad * lowgrad
    corrected_first = new_first / (1.0 - beta_first**adam_step)
    corrected_second = new_second / (1.0 - beta_second**adam_step)
    direction = (corrected_first / (jnp.sqrt(corrected_second) + epsilon)).astype(jnp.bfloat16)
    return (new_first, new_second, direction)


def exchange_sum_kernel(n, part_ref, out_ref, recv, send_sem, recv_sem):
    me = lax.axis_index("dp")
    col = lax.axis_index("tensor")
    barrier = pltpu.get_barrier_semaphore()
    for k in range(1, n):
        pl.semaphore_signal(
            barrier, inc=1, device_id=(lax.rem(me + k, n), col), device_id_type=MESH_ID
        )
    pl.semaphore_wait(barrier, n - 1)
    copies = []
    for k in range(1, n):
        dest = lax.rem(me + k, n)
        copy = pltpu.make_async_remote_copy(
            src_ref=part_ref.at[dest],
            dst_ref=recv.at[k],
            send_sem=send_sem.at[k],
            recv_sem=recv_sem.at[k],
            device_id=(dest, col),
            device_id_type=MESH_ID,
        )
        copy.start()
        copies.append(copy)
    out_ref[...] = part_ref[me].astype(jnp.float32)
    for k, copy in enumerate(copies, 1):
        copy.wait()
        out_ref[...] += recv[k].astype(jnp.float32)


def exchange_sum(part):
    n, rows, cols = part.shape
    return pl.pallas_call(
        functools.partial(exchange_sum_kernel, n),
        out_shape=jax.ShapeDtypeStruct((rows, cols), jnp.float32),
        in_specs=[pl.BlockSpec(memory_space=pltpu.VMEM)],
        out_specs=pl.BlockSpec(memory_space=pltpu.VMEM),
        scratch_shapes=[
            pltpu.VMEM((n, rows, cols), part.dtype),
            pltpu.SemaphoreType.DMA((n,)),
            pltpu.SemaphoreType.DMA((n,)),
        ],
        compiler_params=pltpu.CompilerParams(
            collective_id=0, has_side_effects=True, vmem_limit_bytes=48 * 1024 * 1024
        ),
    )(part)


def per_device(acts, out_grad, projector, weight, first_moment, second_moment):
    token_proj = jnp.dot(acts, projector, preferred_element_type=jnp.float32)
    peers = lax.axis_size("tensor")
    whole_proj = lax.all_to_all(
        jnp.tile(token_proj, (peers, 1)), "tensor", split_axis=0, concat_axis=0, tiled=True
    )
    proj_hi = whole_proj.astype(jnp.bfloat16)
    proj_lo = (whole_proj - proj_hi.astype(jnp.float32)).astype(jnp.bfloat16)
    dims = (((0,), (0,)), ((), ()))
    partial = lax.dot_general(
        out_grad, proj_hi, dims, preferred_element_type=jnp.float32
    ) + lax.dot_general(out_grad, proj_lo, dims, preferred_element_type=jnp.float32)
    owners = lax.axis_size("dp")
    lowgrad = exchange_sum(partial.astype(jnp.bfloat16).reshape(owners, -1, partial.shape[1]))
    new_first, new_second, direction = adam_moments(lowgrad, first_moment[0], second_moment[0])
    owned_update = lax.dot_general(
        projector, direction, (((1,), (1,)), ((), ())), preferred_element_type=jnp.float32
    ).astype(jnp.bfloat16)
    update = lax.all_to_all(owned_update, "dp", split_axis=0, concat_axis=1, tiled=True)
    new_weight = (weight.astype(jnp.float32) - step_rate * update.astype(jnp.float32)).astype(
        jnp.bfloat16
    )
    return (new_weight, new_first[None], new_second[None])


def solution(mesh):
    return jax.shard_map(
        per_device,
        mesh=mesh,
        in_specs=(
            P(("dp", "tensor"), None),
            P("dp", "tensor"),
            P(),
            P("dp", "tensor"),
            P("tensor", "dp", None),
            P("tensor", "dp", None),
        ),
        out_specs=(P("dp", "tensor"), P("tensor", "dp", None), P("tensor", "dp", None)),
        check_vma=False,
    )
```

```python
import functools

import jax
import jax.numpy as jnp
from jax import lax
from jax.experimental import pallas as pl
from jax.experimental.pallas import tpu as pltpu
from jax.sharding import PartitionSpec as P

beta_first = 0.9
beta_second = 0.95
adam_step = 10
epsilon = 1e-08
step_rate = 0.5

MESH_ID = pl.DeviceIdType.MESH


def adam_moments(lowgrad, first_moment, second_moment):
    new_first = beta_first * first_moment + (1.0 - beta_first) * lowgrad
    new_second = beta_second * second_moment + (1.0 - beta_second) * lowgrad * lowgrad
    corrected_first = new_first / (1.0 - beta_first**adam_step)
    corrected_second = new_second / (1.0 - beta_second**adam_step)
    direction = (corrected_first / (jnp.sqrt(corrected_second) + epsilon)).astype(jnp.bfloat16)
    return (new_first, new_second, direction)


def exchange_sum_kernel(n, part_ref, out_ref, recv, send_sem, recv_sem):
    me = lax.axis_index("dp")
    col = lax.axis_index("tensor")
    barrier = pltpu.get_barrier_semaphore()
    for k in range(1, n):
        pl.semaphore_signal(
            barrier, inc=1, device_id=(lax.rem(me + k, n), col), device_id_type=MESH_ID
        )
    pl.semaphore_wait(barrier, n - 1)
    copies = []
    for k in range(1, n):
        dest = lax.rem(me + k, n)
        copy = pltpu.make_async_remote_copy(
            src_ref=part_ref.at[dest],
            dst_ref=recv.at[k],
            send_sem=send_sem.at[k],
            recv_sem=recv_sem.at[k],
            device_id=(dest, col),
            device_id_type=MESH_ID,
        )
        copy.start()
        copies.append(copy)
    out_ref[...] = part_ref[me].astype(jnp.float32)
    for k, copy in enumerate(copies, 1):
        copy.wait()
        out_ref[...] += recv[k].astype(jnp.float32)


def exchange_sum(part):
    n, rows, cols = part.shape
    return pl.pallas_call(
        functools.partial(exchange_sum_kernel, n),
        out_shape=jax.ShapeDtypeStruct((rows, cols), jnp.float32),
        in_specs=[pl.BlockSpec(memory_space=pltpu.VMEM)],
        out_specs=pl.BlockSpec(memory_space=pltpu.VMEM),
        scratch_shapes=[
            pltpu.VMEM((n, rows, cols), part.dtype),
            pltpu.SemaphoreType.DMA((n,)),
            pltpu.SemaphoreType.DMA((n,)),
        ],
        compiler_params=pltpu.CompilerParams(
            collective_id=0, has_side_effects=True, vmem_limit_bytes=48 * 1024 * 1024
        ),
    )(part)


def gather_kernel(n, axis, part_ref, out_ref, recv, send_sem, recv_sem):
    me = lax.axis_index(axis)
    barrier = pltpu.get_barrier_semaphore()
    for k in range(1, n):
        pl.semaphore_signal(
            barrier, inc=1, device_id={axis: lax.rem(me + k, n)}, device_id_type=MESH_ID
        )
    pl.semaphore_wait(barrier, n - 1)
    copies = []
    for k in range(1, n):
        copy = pltpu.make_async_remote_copy(
            src_ref=part_ref,
            dst_ref=recv.at[k],
            send_sem=send_sem.at[k],
            recv_sem=recv_sem.at[k],
            device_id={axis: lax.rem(me + k, n)},
            device_id_type=MESH_ID,
        )
        copy.start()
        copies.append(copy)
    out_ref[me] = part_ref[...]
    for k, copy in enumerate(copies, 1):
        copy.wait()
        out_ref[lax.rem(me + n - k, n)] = recv[k]


def gather(part, axis, n, collective_id):
    return pl.pallas_call(
        functools.partial(gather_kernel, n, axis),
        out_shape=jax.ShapeDtypeStruct((n,) + part.shape, part.dtype),
        in_specs=[pl.BlockSpec(memory_space=pltpu.VMEM)],
        out_specs=pl.BlockSpec(memory_space=pltpu.VMEM),
        scratch_shapes=[
            pltpu.VMEM((n,) + part.shape, part.dtype),
            pltpu.SemaphoreType.DMA((n,)),
            pltpu.SemaphoreType.DMA((n,)),
        ],
        compiler_params=pltpu.CompilerParams(collective_id=collective_id, has_side_effects=True),
    )(part)


def per_device(acts, out_grad, projector, weight, first_moment, second_moment):
    token_proj = jnp.dot(acts, projector, preferred_element_type=jnp.float32)
    peers = lax.axis_size("tensor")
    whole_proj = gather(token_proj, "tensor", peers, 1).reshape(-1, token_proj.shape[1])
    proj_hi = whole_proj.astype(jnp.bfloat16)
    proj_lo = (whole_proj - proj_hi.astype(jnp.float32)).astype(jnp.bfloat16)
    dims = (((0,), (0,)), ((), ()))
    partial = lax.dot_general(
        out_grad, proj_hi, dims, preferred_element_type=jnp.float32
    ) + lax.dot_general(out_grad, proj_lo, dims, preferred_element_type=jnp.float32)
    owners = lax.axis_size("dp")
    blocks = lax.all_to_all(
        partial.astype(jnp.bfloat16).reshape(owners, -1, partial.shape[1]),
        "dp",
        split_axis=0,
        concat_axis=0,
        tiled=True,
    )
    lowgrad = jnp.sum(blocks.astype(jnp.float32), axis=0)
    new_first, new_second, direction = adam_moments(lowgrad, first_moment[0], second_moment[0])
    owned_update = lax.dot_general(
        projector, direction, (((1,), (1,)), ((), ())), preferred_element_type=jnp.float32
    ).astype(jnp.bfloat16)
    update = lax.all_to_all(owned_update, "dp", split_axis=0, concat_axis=1, tiled=True)
    new_weight = (weight.astype(jnp.float32) - step_rate * update.astype(jnp.float32)).astype(
        jnp.bfloat16
    )
    return (new_weight, new_first[None], new_second[None])


def solution(mesh):
    return jax.shard_map(
        per_device,
        mesh=mesh,
        in_specs=(
            P(("dp", "tensor"), None),
            P("dp", "tensor"),
            P(),
            P("dp", "tensor"),
            P("tensor", "dp", None),
            P("tensor", "dp", None),
        ),
        out_specs=(P("dp", "tensor"), P("tensor", "dp", None), P("tensor", "dp", None)),
        check_vma=False,
    )
```

```python
import functools

import jax
import jax.numpy as jnp
from jax import lax
from jax.experimental import pallas as pl
from jax.experimental.pallas import tpu as pltpu
from jax.sharding import PartitionSpec as P

beta_first = 0.9
beta_second = 0.95
adam_step = 10
epsilon = 1e-08
step_rate = 0.5

MESH_ID = pl.DeviceIdType.MESH


def adam_moments(lowgrad, first_moment, second_moment):
    new_first = beta_first * first_moment + (1.0 - beta_first) * lowgrad
    new_second = beta_second * second_moment + (1.0 - beta_second) * lowgrad * lowgrad
    corrected_first = new_first / (1.0 - beta_first**adam_step)
    corrected_second = new_second / (1.0 - beta_second**adam_step)
    direction = (corrected_first / (jnp.sqrt(corrected_second) + epsilon)).astype(jnp.bfloat16)
    return (new_first, new_second, direction)


def tail_kernel(
    n, blocks_ref, first_ref, second_ref, proj_ref, weight_ref,
    new_weight_ref, new_first_ref, new_second_ref,
    total, direction_ref, update, sendbuf, recv, local_sem, send_sem, recv_sem,
):
    me = lax.axis_index("dp")
    col = lax.axis_index("tensor")
    rows = sendbuf.shape[1]
    width = sendbuf.shape[2]
    barrier = pltpu.get_barrier_semaphore()
    for k in range(1, n):
        pl.semaphore_signal(
            barrier, inc=1, device_id=(lax.rem(me + k, n), col), device_id_type=MESH_ID
        )
    pl.semaphore_wait(barrier, n - 1)

    total[...] = blocks_ref[0].astype(jnp.float32)

    def add_block(k, carry):
        total[...] += blocks_ref[k].astype(jnp.float32)
        return carry

    lax.fori_loop(1, n, add_block, 0)
    new_first, new_second, direction = adam_moments(total[...], first_ref[...], second_ref[...])
    new_first_ref[...] = new_first
    new_second_ref[...] = new_second
    direction_ref[...] = direction

    def update_block(j, carry):
        start = pl.multiple_of(j * rows, rows)
        update[j] = lax.dot_general(
            proj_ref[pl.ds(start, rows), :],
            direction_ref[...],
            (((1,), (1,)), ((), ())),
            preferred_element_type=jnp.float32,
        ).astype(jnp.bfloat16)
        return carry

    lax.fori_loop(0, n, update_block, 0)
    local = pltpu.make_async_copy(update, sendbuf, local_sem)
    local.start()
    local.wait()
    copies = []
    for k in range(1, n):
        dest = lax.rem(me + k, n)
        copy = pltpu.make_async_remote_copy(
            src_ref=sendbuf.at[dest],
            dst_ref=recv.at[k],
            send_sem=send_sem.at[k],
            recv_sem=recv_sem.at[k],
            device_id=(dest, col),
            device_id_type=MESH_ID,
        )
        copy.start()
        copies.append(copy)

    def apply(source, block):
        cols = pl.ds(pl.multiple_of(source * width, width), width)
        new_weight_ref[:, cols] = (
            weight_ref[:, cols].astype(jnp.float32) - step_rate * block.astype(jnp.float32)
        ).astype(jnp.bfloat16)

    apply(me, sendbuf[me])
    for k, copy in enumerate(copies, 1):
        copy.wait()
        apply(lax.rem(me + n - k, n), recv[k])


def tail(blocks, first_moment, second_moment, projector, weight):
    n, hidden, rank = blocks.shape
    rows = weight.shape[0]
    vmem = pl.BlockSpec(memory_space=pltpu.VMEM)
    return pl.pallas_call(
        functools.partial(tail_kernel, n),
        out_shape=(
            jax.ShapeDtypeStruct(weight.shape, weight.dtype),
            jax.ShapeDtypeStruct((hidden, rank), jnp.float32),
            jax.ShapeDtypeStruct((hidden, rank), jnp.float32),
        ),
        in_specs=[vmem] * 5,
        out_specs=(vmem, vmem, vmem),
        scratch_shapes=[
            pltpu.VMEM((hidden, rank), jnp.float32),
            pltpu.VMEM((hidden, rank), jnp.bfloat16),
            pltpu.VMEM((n, rows, hidden), jnp.bfloat16),
            pltpu.VMEM((n, rows, hidden), jnp.bfloat16),
            pltpu.VMEM((n, rows, hidden), jnp.bfloat16),
            pltpu.SemaphoreType.DMA(()),
            pltpu.SemaphoreType.DMA((n,)),
            pltpu.SemaphoreType.DMA((n,)),
        ],
        compiler_params=pltpu.CompilerParams(
            collective_id=2, has_side_effects=True, vmem_limit_bytes=48 * 1024 * 1024
        ),
    )(blocks, first_moment, second_moment, projector, weight)


def per_device(acts, out_grad, projector, weight, first_moment, second_moment):
    token_proj = jnp.dot(acts, projector, preferred_element_type=jnp.float32)
    peers = lax.axis_size("tensor")
    whole_proj = lax.all_to_all(
        jnp.tile(token_proj, (peers, 1)), "tensor", split_axis=0, concat_axis=0, tiled=True
    )
    proj_hi = whole_proj.astype(jnp.bfloat16)
    proj_lo = (whole_proj - proj_hi.astype(jnp.float32)).astype(jnp.bfloat16)
    dims = (((0,), (0,)), ((), ()))
    partial = lax.dot_general(
        out_grad, proj_hi, dims, preferred_element_type=jnp.float32
    ) + lax.dot_general(out_grad, proj_lo, dims, preferred_element_type=jnp.float32)
    owners = lax.axis_size("dp")
    blocks = lax.all_to_all(
        partial.astype(jnp.bfloat16).reshape(owners, -1, partial.shape[1]),
        "dp",
        split_axis=0,
        concat_axis=0,
        tiled=True,
    )
    new_weight, new_first, new_second = tail(
        blocks, first_moment[0], second_moment[0], projector, weight
    )
    return (new_weight, new_first[None], new_second[None])


def solution(mesh):
    return jax.shard_map(
        per_device,
        mesh=mesh,
        in_specs=(
            P(("dp", "tensor"), None),
            P("dp", "tensor"),
            P(),
            P("dp", "tensor"),
            P("tensor", "dp", None),
            P("tensor", "dp", None),
        ),
        out_specs=(P("dp", "tensor"), P("tensor", "dp", None), P("tensor", "dp", None)),
        check_vma=False,
    )
```

```python
import functools

import jax
import jax.numpy as jnp
from jax import lax
from jax.experimental import pallas as pl
from jax.experimental.pallas import tpu as pltpu
from jax.sharding import PartitionSpec as P

beta_first = 0.9
beta_second = 0.95
adam_step = 10
epsilon = 1e-08
step_rate = 0.5

MESH_ID = pl.DeviceIdType.MESH


def adam_moments(lowgrad, first_moment, second_moment):
    new_first = beta_first * first_moment + (1.0 - beta_first) * lowgrad
    new_second = beta_second * second_moment + (1.0 - beta_second) * lowgrad * lowgrad
    corrected_first = new_first / (1.0 - beta_first**adam_step)
    corrected_second = new_second / (1.0 - beta_second**adam_step)
    direction = (corrected_first / (jnp.sqrt(corrected_second) + epsilon)).astype(jnp.bfloat16)
    return (new_first, new_second, direction)


def tail_kernel(
    n, blocks_ref, first_ref, second_ref, proj_ref, weight_ref,
    new_weight_ref, new_first_ref, new_second_ref,
    total, direction_ref, update, sendbuf, recv, local_sem, send_sem, recv_sem,
):
    me = lax.axis_index("dp")
    col = lax.axis_index("tensor")
    rows = sendbuf.shape[1]
    width = sendbuf.shape[2]
    barrier = pltpu.get_barrier_semaphore()
    for k in range(1, n):
        pl.semaphore_signal(
            barrier, inc=1, device_id=(lax.rem(me + k, n), col), device_id_type=MESH_ID
        )
    pl.semaphore_wait(barrier, n - 1)

    total[...] = blocks_ref[0].astype(jnp.float32)

    def add_block(k, carry):
        total[...] += blocks_ref[k].astype(jnp.float32)
        return carry

    lax.fori_loop(1, n, add_block, 0)
    new_first, new_second, direction = adam_moments(total[...], first_ref[...], second_ref[...])
    new_first_ref[...] = new_first
    new_second_ref[...] = new_second
    direction_ref[...] = direction

    def update_block(j, carry):
        start = pl.multiple_of(j * rows, rows)
        update[j] = lax.dot_general(
            proj_ref[pl.ds(start, rows), :],
            direction_ref[...],
            (((1,), (1,)), ((), ())),
            preferred_element_type=jnp.float32,
        ).astype(jnp.bfloat16)
        return carry

    lax.fori_loop(0, n, update_block, 0)
    local = pltpu.make_async_copy(update, sendbuf, local_sem)
    local.start()
    local.wait()
    copies = []
    for k in range(1, n):
        dest = lax.rem(me + k, n)
        copy = pltpu.make_async_remote_copy(
            src_ref=sendbuf.at[dest],
            dst_ref=recv.at[k],
            send_sem=send_sem.at[k],
            recv_sem=recv_sem.at[k],
            device_id=(dest, col),
            device_id_type=MESH_ID,
        )
        copy.start()
        copies.append(copy)

    def apply(source, block):
        cols = pl.ds(pl.multiple_of(source * width, width), width)
        new_weight_ref[:, cols] = (
            weight_ref[:, cols].astype(jnp.float32) - step_rate * block.astype(jnp.float32)
        ).astype(jnp.bfloat16)

    apply(me, sendbuf[me])
    for k, copy in enumerate(copies, 1):
        copy.wait()
        apply(lax.rem(me + n - k, n), recv[k])


def tail(blocks, first_moment, second_moment, projector, weight):
    n, hidden, rank = blocks.shape
    rows = weight.shape[0]
    vmem = pl.BlockSpec(memory_space=pltpu.VMEM)
    return pl.pallas_call(
        functools.partial(tail_kernel, n),
        out_shape=(
            jax.ShapeDtypeStruct(weight.shape, weight.dtype),
            jax.ShapeDtypeStruct((hidden, rank), jnp.float32),
            jax.ShapeDtypeStruct((hidden, rank), jnp.float32),
        ),
        in_specs=[vmem] * 5,
        out_specs=(vmem, vmem, vmem),
        scratch_shapes=[
            pltpu.VMEM((hidden, rank), jnp.float32),
            pltpu.VMEM((hidden, rank), jnp.bfloat16),
            pltpu.VMEM((n, rows, hidden), jnp.bfloat16),
            pltpu.VMEM((n, rows, hidden), jnp.bfloat16),
            pltpu.VMEM((n, rows, hidden), jnp.bfloat16),
            pltpu.SemaphoreType.DMA(()),
            pltpu.SemaphoreType.DMA((n,)),
            pltpu.SemaphoreType.DMA((n,)),
        ],
        compiler_params=pltpu.CompilerParams(
            collective_id=2, has_side_effects=True, vmem_limit_bytes=48 * 1024 * 1024
        ),
    )(blocks, first_moment, second_moment, projector, weight)


def per_device(acts, out_grad, projector, weight, first_moment, second_moment):
    token_proj = jnp.dot(acts, projector, preferred_element_type=jnp.float32)
    peers = lax.axis_size("tensor")
    whole_proj = lax.all_to_all(
        jnp.tile(token_proj, (peers, 1)), "tensor", split_axis=0, concat_axis=0, tiled=True
    )
    proj_hi = whole_proj.astype(jnp.bfloat16)
    proj_lo = (whole_proj - proj_hi.astype(jnp.float32)).astype(jnp.bfloat16)
    owners = lax.axis_size("dp")
    grad_blocks = out_grad.reshape(out_grad.shape[0], owners, -1)
    dims = (((0,), (0,)), ((), ()))
    partial = lax.dot_general(
        grad_blocks, proj_hi, dims, preferred_element_type=jnp.float32
    ) + lax.dot_general(grad_blocks, proj_lo, dims, preferred_element_type=jnp.float32)
    blocks = lax.all_to_all(
        partial.astype(jnp.bfloat16), "dp", split_axis=0, concat_axis=0, tiled=True
    )
    new_weight, new_first, new_second = tail(
        blocks, first_moment[0], second_moment[0], projector, weight
    )
    return (new_weight, new_first[None], new_second[None])


def solution(mesh):
    return jax.shard_map(
        per_device,
        mesh=mesh,
        in_specs=(
            P(("dp", "tensor"), None),
            P("dp", "tensor"),
            P(),
            P("dp", "tensor"),
            P("tensor", "dp", None),
            P("tensor", "dp", None),
        ),
        out_specs=(P("dp", "tensor"), P("tensor", "dp", None), P("tensor", "dp", None)),
        check_vma=False,
    )
```

```python
import functools

import jax
import jax.numpy as jnp
from jax import lax
from jax.experimental import pallas as pl
from jax.experimental.pallas import tpu as pltpu
from jax.sharding import PartitionSpec as P

beta_first = 0.9
beta_second = 0.95
adam_step = 10
epsilon = 1e-08
step_rate = 0.5

MESH_ID = pl.DeviceIdType.MESH


def adam_moments(lowgrad, first_moment, second_moment):
    new_first = beta_first * first_moment + (1.0 - beta_first) * lowgrad
    new_second = beta_second * second_moment + (1.0 - beta_second) * lowgrad * lowgrad
    corrected_first = new_first / (1.0 - beta_first**adam_step)
    corrected_second = new_second / (1.0 - beta_second**adam_step)
    direction = (corrected_first / (jnp.sqrt(corrected_second) + epsilon)).astype(jnp.bfloat16)
    return (new_first, new_second, direction)


def tail_kernel(
    n, blocks_ref, first_ref, second_ref, proj_ref, weight_ref,
    new_weight_ref, new_first_ref, new_second_ref,
    total, direction_ref, update, sendbuf, recv, local_sem, send_sem, recv_sem,
):
    me = lax.axis_index("dp")
    col = lax.axis_index("tensor")
    rows = sendbuf.shape[1]
    width = sendbuf.shape[2]
    barrier = pltpu.get_barrier_semaphore()
    for k in range(1, n):
        pl.semaphore_signal(
            barrier, inc=1, device_id=(lax.rem(me + k, n), col), device_id_type=MESH_ID
        )
    pl.semaphore_wait(barrier, n - 1)

    total[...] = blocks_ref[0].astype(jnp.float32)

    def add_block(k, carry):
        total[...] += blocks_ref[k].astype(jnp.float32)
        return carry

    lax.fori_loop(1, n, add_block, 0)
    new_first, new_second, direction = adam_moments(total[...], first_ref[...], second_ref[...])
    new_first_ref[...] = new_first
    new_second_ref[...] = new_second
    direction_ref[...] = direction

    def update_block(j, carry):
        start = pl.multiple_of(j * rows, rows)
        update[j] = lax.dot_general(
            proj_ref[pl.ds(start, rows), :],
            direction_ref[...],
            (((1,), (1,)), ((), ())),
            preferred_element_type=jnp.float32,
        ).astype(jnp.bfloat16)
        return carry

    lax.fori_loop(0, n, update_block, 0)
    local = pltpu.make_async_copy(update, sendbuf, local_sem)
    local.start()
    local.wait()
    copies = []
    for k in range(1, n):
        dest = lax.rem(me + k, n)
        copy = pltpu.make_async_remote_copy(
            src_ref=sendbuf.at[dest],
            dst_ref=recv.at[k],
            send_sem=send_sem.at[k],
            recv_sem=recv_sem.at[k],
            device_id=(dest, col),
            device_id_type=MESH_ID,
        )
        copy.start()
        copies.append(copy)

    def apply(source, block):
        cols = pl.ds(pl.multiple_of(source * width, width), width)
        new_weight_ref[:, cols] = (
            weight_ref[:, cols].astype(jnp.float32) - step_rate * block.astype(jnp.float32)
        ).astype(jnp.bfloat16)

    apply(me, sendbuf[me])
    for k, copy in enumerate(copies, 1):
        copy.wait()
        apply(lax.rem(me + n - k, n), recv[k])


def tail(blocks, first_moment, second_moment, projector, weight):
    n, hidden, rank = blocks.shape
    rows = weight.shape[0]
    vmem = pl.BlockSpec(memory_space=pltpu.VMEM)
    return pl.pallas_call(
        functools.partial(tail_kernel, n),
        out_shape=(
            jax.ShapeDtypeStruct(weight.shape, weight.dtype),
            jax.ShapeDtypeStruct((hidden, rank), jnp.float32),
            jax.ShapeDtypeStruct((hidden, rank), jnp.float32),
        ),
        in_specs=[vmem] * 5,
        out_specs=(vmem, vmem, vmem),
        scratch_shapes=[
            pltpu.VMEM((hidden, rank), jnp.float32),
            pltpu.VMEM((hidden, rank), jnp.bfloat16),
            pltpu.VMEM((n, rows, hidden), jnp.bfloat16),
            pltpu.VMEM((n, rows, hidden), jnp.bfloat16),
            pltpu.VMEM((n, rows, hidden), jnp.bfloat16),
            pltpu.SemaphoreType.DMA(()),
            pltpu.SemaphoreType.DMA((n,)),
            pltpu.SemaphoreType.DMA((n,)),
        ],
        compiler_params=pltpu.CompilerParams(
            collective_id=2, has_side_effects=True, vmem_limit_bytes=48 * 1024 * 1024
        ),
    )(blocks, first_moment, second_moment, projector, weight)


def chip_gather_kernel(q_ref, out_ref, recv, send_sem, recv_sem):
    me = lax.axis_index("tensor")
    core_peer = me + 1 - 2 * lax.rem(me, 2)
    chip_peer = lax.rem(me + 2, 4)
    barrier = pltpu.get_barrier_semaphore()
    for peer in (core_peer, chip_peer):
        pl.semaphore_signal(barrier, inc=1, device_id={"tensor": peer}, device_id_type=MESH_ID)
    pl.semaphore_wait(barrier, 2)

    def send(src, slot, peer):
        copy = pltpu.make_async_remote_copy(
            src_ref=src,
            dst_ref=recv.at[slot],
            send_sem=send_sem.at[slot],
            recv_sem=recv_sem.at[slot],
            device_id={"tensor": peer},
            device_id_type=MESH_ID,
        )
        copy.start()
        return copy

    across = send(q_ref, 1, chip_peer)
    beside = send(q_ref, 0, core_peer)
    out_ref[me] = q_ref[...]
    across.wait()
    forward = send(recv.at[1], 2, core_peer)
    out_ref[chip_peer] = recv[1]
    beside.wait()
    out_ref[core_peer] = recv[0]
    forward.wait()
    out_ref[3 - me] = recv[2]


def chip_gather(q):
    return pl.pallas_call(
        chip_gather_kernel,
        out_shape=jax.ShapeDtypeStruct((4,) + q.shape, q.dtype),
        in_specs=[pl.BlockSpec(memory_space=pltpu.VMEM)],
        out_specs=pl.BlockSpec(memory_space=pltpu.VMEM),
        scratch_shapes=[
            pltpu.VMEM((3,) + q.shape, q.dtype),
            pltpu.SemaphoreType.DMA((3,)),
            pltpu.SemaphoreType.DMA((3,)),
        ],
        compiler_params=pltpu.CompilerParams(collective_id=1, has_side_effects=True),
    )(q)


def per_device(acts, out_grad, projector, weight, first_moment, second_moment):
    token_proj = jnp.dot(acts, projector, preferred_element_type=jnp.float32)
    assert lax.axis_size("tensor") == 4
    whole_proj = chip_gather(token_proj).reshape(-1, token_proj.shape[1])
    proj_hi = whole_proj.astype(jnp.bfloat16)
    proj_lo = (whole_proj - proj_hi.astype(jnp.float32)).astype(jnp.bfloat16)
    owners = lax.axis_size("dp")
    grad_blocks = out_grad.reshape(out_grad.shape[0], owners, -1)
    dims = (((0,), (0,)), ((), ()))
    partial = lax.dot_general(
        grad_blocks, proj_hi, dims, preferred_element_type=jnp.float32
    ) + lax.dot_general(grad_blocks, proj_lo, dims, preferred_element_type=jnp.float32)
    blocks = lax.all_to_all(
        partial.astype(jnp.bfloat16), "dp", split_axis=0, concat_axis=0, tiled=True
    )
    new_weight, new_first, new_second = tail(
        blocks, first_moment[0], second_moment[0], projector, weight
    )
    return (new_weight, new_first[None], new_second[None])


def solution(mesh):
    return jax.shard_map(
        per_device,
        mesh=mesh,
        in_specs=(
            P(("dp", "tensor"), None),
            P("dp", "tensor"),
            P(),
            P("dp", "tensor"),
            P("tensor", "dp", None),
            P("tensor", "dp", None),
        ),
        out_specs=(P("dp", "tensor"), P("tensor", "dp", None), P("tensor", "dp", None)),
        check_vma=False,
    )
```

```python
import functools

import jax
import jax.numpy as jnp
from jax import lax
from jax.experimental import pallas as pl
from jax.experimental.pallas import tpu as pltpu
from jax.sharding import PartitionSpec as P

beta_first = 0.9
beta_second = 0.95
adam_step = 10
epsilon = 1e-08
step_rate = 0.5

MESH_ID = pl.DeviceIdType.MESH


def adam_moments(lowgrad, first_moment, second_moment):
    new_first = beta_first * first_moment + (1.0 - beta_first) * lowgrad
    new_second = beta_second * second_moment + (1.0 - beta_second) * lowgrad * lowgrad
    corrected_first = new_first / (1.0 - beta_first**adam_step)
    corrected_second = new_second / (1.0 - beta_second**adam_step)
    direction = (corrected_first / (jnp.sqrt(corrected_second) + epsilon)).astype(jnp.bfloat16)
    return (new_first, new_second, direction)


def tail_kernel(
    n, blocks_ref, first_ref, second_ref, proj_ref, weight_ref,
    new_weight_ref, new_first_ref, new_second_ref,
    total, direction_ref, update, sendbuf, recv, local_sem, send_sem, recv_sem,
):
    me = lax.axis_index("dp")
    col = lax.axis_index("tensor")
    rows = sendbuf.shape[1]
    width = sendbuf.shape[2]
    barrier = pltpu.get_barrier_semaphore()
    for k in range(1, n):
        pl.semaphore_signal(
            barrier, inc=1, device_id=(lax.rem(me + k, n), col), device_id_type=MESH_ID
        )

    total[...] = blocks_ref[0].astype(jnp.float32)

    def add_block(k, carry):
        total[...] += blocks_ref[k].astype(jnp.float32)
        return carry

    lax.fori_loop(1, n, add_block, 0)
    new_first, new_second, direction = adam_moments(total[...], first_ref[...], second_ref[...])
    new_first_ref[...] = new_first
    new_second_ref[...] = new_second
    direction_ref[...] = direction

    update[...] = (
        lax.dot_general(
            proj_ref[...],
            direction_ref[...],
            (((1,), (1,)), ((), ())),
            preferred_element_type=jnp.float32,
        )
        .astype(jnp.bfloat16)
        .reshape(update.shape)
    )
    local = pltpu.make_async_copy(update, sendbuf, local_sem)
    local.start()
    local.wait()
    pl.semaphore_wait(barrier, n - 1)
    copies = []
    for k in range(1, n):
        dest = lax.rem(me + k, n)
        copy = pltpu.make_async_remote_copy(
            src_ref=sendbuf.at[dest],
            dst_ref=recv.at[k],
            send_sem=send_sem.at[k],
            recv_sem=recv_sem.at[k],
            device_id=(dest, col),
            device_id_type=MESH_ID,
        )
        copy.start()
        copies.append(copy)

    def apply(source, block):
        cols = pl.ds(pl.multiple_of(source * width, width), width)
        new_weight_ref[:, cols] = (
            weight_ref[:, cols].astype(jnp.float32) - step_rate * block.astype(jnp.float32)
        ).astype(jnp.bfloat16)

    apply(me, sendbuf[me])
    for k, copy in enumerate(copies, 1):
        copy.wait()
        apply(lax.rem(me + n - k, n), recv[k])


def tail(blocks, first_moment, second_moment, projector, weight):
    n, hidden, rank = blocks.shape
    rows = weight.shape[0]
    vmem = pl.BlockSpec(memory_space=pltpu.VMEM)
    return pl.pallas_call(
        functools.partial(tail_kernel, n),
        out_shape=(
            jax.ShapeDtypeStruct(weight.shape, weight.dtype),
            jax.ShapeDtypeStruct((hidden, rank), jnp.float32),
            jax.ShapeDtypeStruct((hidden, rank), jnp.float32),
        ),
        in_specs=[vmem] * 5,
        out_specs=(vmem, vmem, vmem),
        scratch_shapes=[
            pltpu.VMEM((hidden, rank), jnp.float32),
            pltpu.VMEM((hidden, rank), jnp.bfloat16),
            pltpu.VMEM((n, rows, hidden), jnp.bfloat16),
            pltpu.VMEM((n, rows, hidden), jnp.bfloat16),
            pltpu.VMEM((n, rows, hidden), jnp.bfloat16),
            pltpu.SemaphoreType.DMA(()),
            pltpu.SemaphoreType.DMA((n,)),
            pltpu.SemaphoreType.DMA((n,)),
        ],
        compiler_params=pltpu.CompilerParams(
            collective_id=2, has_side_effects=True, vmem_limit_bytes=48 * 1024 * 1024
        ),
    )(blocks, first_moment, second_moment, projector, weight)


def chip_gather_kernel(q_ref, out_ref, recv, send_sem, recv_sem):
    me = lax.axis_index("tensor")
    core_peer = me + 1 - 2 * lax.rem(me, 2)
    chip_peer = lax.rem(me + 2, 4)
    barrier = pltpu.get_barrier_semaphore()
    for peer in (core_peer, chip_peer):
        pl.semaphore_signal(barrier, inc=1, device_id={"tensor": peer}, device_id_type=MESH_ID)
    pl.semaphore_wait(barrier, 2)

    def send(src, slot, peer):
        copy = pltpu.make_async_remote_copy(
            src_ref=src,
            dst_ref=recv.at[slot],
            send_sem=send_sem.at[slot],
            recv_sem=recv_sem.at[slot],
            device_id={"tensor": peer},
            device_id_type=MESH_ID,
        )
        copy.start()
        return copy

    across = send(q_ref, 1, chip_peer)
    beside = send(q_ref, 0, core_peer)
    out_ref[me] = q_ref[...]
    across.wait()
    forward = send(recv.at[1], 2, core_peer)
    out_ref[chip_peer] = recv[1]
    beside.wait()
    out_ref[core_peer] = recv[0]
    forward.wait()
    out_ref[3 - me] = recv[2]


def chip_gather(q):
    return pl.pallas_call(
        chip_gather_kernel,
        out_shape=jax.ShapeDtypeStruct((4,) + q.shape, q.dtype),
        in_specs=[pl.BlockSpec(memory_space=pltpu.VMEM)],
        out_specs=pl.BlockSpec(memory_space=pltpu.VMEM),
        scratch_shapes=[
            pltpu.VMEM((3,) + q.shape, q.dtype),
            pltpu.SemaphoreType.DMA((3,)),
            pltpu.SemaphoreType.DMA((3,)),
        ],
        compiler_params=pltpu.CompilerParams(collective_id=1, has_side_effects=True),
    )(q)


def per_device(acts, out_grad, projector, weight, first_moment, second_moment):
    token_proj = jnp.dot(acts, projector, preferred_element_type=jnp.float32)
    assert lax.axis_size("tensor") == 4
    whole_proj = chip_gather(token_proj).reshape(-1, token_proj.shape[1])
    proj_hi = whole_proj.astype(jnp.bfloat16)
    proj_lo = (whole_proj - proj_hi.astype(jnp.float32)).astype(jnp.bfloat16)
    owners = lax.axis_size("dp")
    grad_blocks = out_grad.reshape(out_grad.shape[0], owners, -1)
    dims = (((0,), (0,)), ((), ()))
    partial = lax.dot_general(
        grad_blocks, proj_hi, dims, preferred_element_type=jnp.float32
    ) + lax.dot_general(grad_blocks, proj_lo, dims, preferred_element_type=jnp.float32)
    blocks = lax.all_to_all(
        partial.astype(jnp.bfloat16), "dp", split_axis=0, concat_axis=0, tiled=True
    )
    new_weight, new_first, new_second = tail(
        blocks, first_moment[0], second_moment[0], projector, weight
    )
    return (new_weight, new_first[None], new_second[None])


def solution(mesh):
    return jax.shard_map(
        per_device,
        mesh=mesh,
        in_specs=(
            P(("dp", "tensor"), None),
            P("dp", "tensor"),
            P(),
            P("dp", "tensor"),
            P("tensor", "dp", None),
            P("tensor", "dp", None),
        ),
        out_specs=(P("dp", "tensor"), P("tensor", "dp", None), P("tensor", "dp", None)),
        check_vma=False,
    )
```

```python
import functools

import jax
import jax.numpy as jnp
from jax import lax
from jax.experimental import pallas as pl
from jax.experimental.pallas import tpu as pltpu
from jax.sharding import PartitionSpec as P

beta_first = 0.9
beta_second = 0.95
adam_step = 10
epsilon = 1e-08
step_rate = 0.5

MESH_ID = pl.DeviceIdType.MESH


def adam_moments(lowgrad, first_moment, second_moment):
    new_first = beta_first * first_moment + (1.0 - beta_first) * lowgrad
    new_second = beta_second * second_moment + (1.0 - beta_second) * lowgrad * lowgrad
    corrected_first = new_first / (1.0 - beta_first**adam_step)
    corrected_second = new_second / (1.0 - beta_second**adam_step)
    direction = (corrected_first / (jnp.sqrt(corrected_second) + epsilon)).astype(jnp.bfloat16)
    return (new_first, new_second, direction)


def tail_kernel(
    n, blocks_ref, first_ref, second_ref, proj_ref, weight_ref,
    new_weight_ref, new_first_ref, new_second_ref,
    total, direction_ref, update, sendbuf, recv, local_sem, send_sem, recv_sem,
):
    me = lax.axis_index("dp")
    col = lax.axis_index("tensor")
    rows = sendbuf.shape[1]
    width = sendbuf.shape[2]
    barrier = pltpu.get_barrier_semaphore()
    for k in range(1, n):
        pl.semaphore_signal(
            barrier, inc=1, device_id=(lax.rem(me + k, n), col), device_id_type=MESH_ID
        )

    total[...] = blocks_ref[0].astype(jnp.float32)

    def add_block(k, carry):
        total[...] += blocks_ref[k].astype(jnp.float32)
        return carry

    lax.fori_loop(1, n, add_block, 0)
    new_first, new_second, direction = adam_moments(total[...], first_ref[...], second_ref[...])
    new_first_ref[...] = new_first
    new_second_ref[...] = new_second
    direction_ref[...] = direction

    update[...] = (
        lax.dot_general(
            proj_ref[...],
            direction_ref[...],
            (((1,), (1,)), ((), ())),
            preferred_element_type=jnp.float32,
        )
        .astype(jnp.bfloat16)
        .reshape(update.shape)
    )
    local = pltpu.make_async_copy(update, sendbuf, local_sem)
    local.start()
    local.wait()
    pl.semaphore_wait(barrier, n - 1)
    copies = []
    for k in range(1, n):
        dest = lax.rem(me + k, n)
        copy = pltpu.make_async_remote_copy(
            src_ref=sendbuf.at[dest],
            dst_ref=recv.at[k],
            send_sem=send_sem.at[k],
            recv_sem=recv_sem.at[k],
            device_id=(dest, col),
            device_id_type=MESH_ID,
        )
        copy.start()
        copies.append(copy)

    def apply(source, block):
        cols = pl.ds(pl.multiple_of(source * width, width), width)
        new_weight_ref[:, cols] = (
            weight_ref[:, cols].astype(jnp.float32) - step_rate * block.astype(jnp.float32)
        ).astype(jnp.bfloat16)

    apply(me, sendbuf[me])
    for k, copy in enumerate(copies, 1):
        copy.wait()
        apply(lax.rem(me + n - k, n), recv[k])


def tail(blocks, first_moment, second_moment, projector, weight):
    n, hidden, rank = blocks.shape
    rows = weight.shape[0]
    vmem = pl.BlockSpec(memory_space=pltpu.VMEM)
    return pl.pallas_call(
        functools.partial(tail_kernel, n),
        out_shape=(
            jax.ShapeDtypeStruct(weight.shape, weight.dtype),
            jax.ShapeDtypeStruct((hidden, rank), jnp.float32),
            jax.ShapeDtypeStruct((hidden, rank), jnp.float32),
        ),
        in_specs=[vmem] * 5,
        out_specs=(vmem, vmem, vmem),
        scratch_shapes=[
            pltpu.VMEM((hidden, rank), jnp.float32),
            pltpu.VMEM((hidden, rank), jnp.bfloat16),
            pltpu.VMEM((n, rows, hidden), jnp.bfloat16),
            pltpu.VMEM((n, rows, hidden), jnp.bfloat16),
            pltpu.VMEM((n, rows, hidden), jnp.bfloat16),
            pltpu.SemaphoreType.DMA(()),
            pltpu.SemaphoreType.DMA((n,)),
            pltpu.SemaphoreType.DMA((n,)),
        ],
        compiler_params=pltpu.CompilerParams(
            collective_id=2, has_side_effects=True, vmem_limit_bytes=48 * 1024 * 1024
        ),
    )(blocks, first_moment, second_moment, projector, weight)


def chip_gather_kernel(
    acts_ref, proj_ref, hi_ref, lo_ref, q_buf, send_buf, recv, local_sem, send_sem, recv_sem
):
    me = lax.axis_index("tensor")
    core_peer = me + 1 - 2 * lax.rem(me, 2)
    chip_peer = lax.rem(me + 2, 4)
    barrier = pltpu.get_barrier_semaphore()
    for peer in (core_peer, chip_peer):
        pl.semaphore_signal(barrier, inc=1, device_id={"tensor": peer}, device_id_type=MESH_ID)
    q_buf[...] = jnp.dot(acts_ref[...], proj_ref[...], preferred_element_type=jnp.float32)
    local = pltpu.make_async_copy(q_buf, send_buf, local_sem)
    local.start()
    local.wait()
    pl.semaphore_wait(barrier, 2)

    def send(src, slot, peer):
        copy = pltpu.make_async_remote_copy(
            src_ref=src,
            dst_ref=recv.at[slot],
            send_sem=send_sem.at[slot],
            recv_sem=recv_sem.at[slot],
            device_id={"tensor": peer},
            device_id_type=MESH_ID,
        )
        copy.start()
        return copy

    def split(slot, piece):
        hi = piece.astype(jnp.bfloat16)
        hi_ref[slot] = hi
        lo_ref[slot] = (piece - hi.astype(jnp.float32)).astype(jnp.bfloat16)

    across = send(send_buf, 1, chip_peer)
    beside = send(send_buf, 0, core_peer)
    split(me, send_buf[...])
    across.wait()
    forward = send(recv.at[1], 2, core_peer)
    split(chip_peer, recv[1])
    beside.wait()
    split(core_peer, recv[0])
    forward.wait()
    split(3 - me, recv[2])


def chip_gather(acts, projector):
    shape = (acts.shape[0], projector.shape[1])
    vmem = pl.BlockSpec(memory_space=pltpu.VMEM)
    return pl.pallas_call(
        chip_gather_kernel,
        out_shape=(
            jax.ShapeDtypeStruct((4,) + shape, jnp.bfloat16),
            jax.ShapeDtypeStruct((4,) + shape, jnp.bfloat16),
        ),
        in_specs=[vmem, vmem],
        out_specs=(vmem, vmem),
        scratch_shapes=[
            pltpu.VMEM(shape, jnp.float32),
            pltpu.VMEM(shape, jnp.float32),
            pltpu.VMEM((3,) + shape, jnp.float32),
            pltpu.SemaphoreType.DMA(()),
            pltpu.SemaphoreType.DMA((3,)),
            pltpu.SemaphoreType.DMA((3,)),
        ],
        compiler_params=pltpu.CompilerParams(
            collective_id=1, has_side_effects=True, vmem_limit_bytes=48 * 1024 * 1024
        ),
    )(acts, projector)


def per_device(acts, out_grad, projector, weight, first_moment, second_moment):
    assert lax.axis_size("tensor") == 4
    proj_hi, proj_lo = chip_gather(acts, projector)
    proj_hi = proj_hi.reshape(-1, proj_hi.shape[2])
    proj_lo = proj_lo.reshape(-1, proj_lo.shape[2])
    owners = lax.axis_size("dp")
    grad_blocks = out_grad.reshape(out_grad.shape[0], owners, -1)
    dims = (((0,), (0,)), ((), ()))
    partial = lax.dot_general(
        grad_blocks, proj_hi, dims, preferred_element_type=jnp.float32
    ) + lax.dot_general(grad_blocks, proj_lo, dims, preferred_element_type=jnp.float32)
    blocks = lax.all_to_all(
        partial.astype(jnp.bfloat16), "dp", split_axis=0, concat_axis=0, tiled=True
    )
    new_weight, new_first, new_second = tail(
        blocks, first_moment[0], second_moment[0], projector, weight
    )
    return (new_weight, new_first[None], new_second[None])


def solution(mesh):
    return jax.shard_map(
        per_device,
        mesh=mesh,
        in_specs=(
            P(("dp", "tensor"), None),
            P("dp", "tensor"),
            P(),
            P("dp", "tensor"),
            P("tensor", "dp", None),
            P("tensor", "dp", None),
        ),
        out_specs=(P("dp", "tensor"), P("tensor", "dp", None), P("tensor", "dp", None)),
        check_vma=False,
    )
```

```python
import functools

import jax
import jax.numpy as jnp
from jax import lax
from jax.experimental import pallas as pl
from jax.experimental.pallas import tpu as pltpu
from jax.sharding import PartitionSpec as P

beta_first = 0.9
beta_second = 0.95
adam_step = 10
epsilon = 1e-08
step_rate = 0.5

MESH_ID = pl.DeviceIdType.MESH


def adam_moments(lowgrad, first_moment, second_moment):
    new_first = beta_first * first_moment + (1.0 - beta_first) * lowgrad
    new_second = beta_second * second_moment + (1.0 - beta_second) * lowgrad * lowgrad
    corrected_first = new_first / (1.0 - beta_first**adam_step)
    corrected_second = new_second / (1.0 - beta_second**adam_step)
    direction = (corrected_first / (jnp.sqrt(corrected_second) + epsilon)).astype(jnp.bfloat16)
    return (new_first, new_second, direction)


def step_kernel(
    n, pieces, grad_ref, hi_ref, lo_ref, first_ref, second_ref, proj_ref, weight_ref,
    new_weight_ref, new_first_ref, new_second_ref,
    part, part_out, blocks, total, direction_ref, update, sendbuf, recv,
    local_sem, part_send, part_recv, send_sem, recv_sem,
):
    me = lax.axis_index("dp")
    col = lax.axis_index("tensor")
    owned = part.shape[1]
    rows = sendbuf.shape[1]
    width = sendbuf.shape[2]
    barrier = pltpu.get_barrier_semaphore()
    for k in range(1, n):
        pl.semaphore_signal(
            barrier, inc=1, device_id=(lax.rem(me + k, n), col), device_id_type=MESH_ID
        )

    def partial_block(j, carry):
        grad = grad_ref[:, pl.ds(pl.multiple_of(j * owned, owned), owned)]
        dims = (((0,), (0,)), ((), ()))
        term = lax.dot_general(grad, hi_ref[...], dims, preferred_element_type=jnp.float32)
        term += lax.dot_general(grad, lo_ref[...], dims, preferred_element_type=jnp.float32)
        part[j] = term.astype(jnp.bfloat16)
        return carry

    lax.fori_loop(0, n, partial_block, 0)
    local = pltpu.make_async_copy(part, part_out, local_sem)
    local.start()
    local.wait()
    pl.semaphore_wait(barrier, n - 1)
    piece = owned // pieces

    def part_copy(k, p):
        dest = lax.rem(me + k, n)
        span = pl.ds(pl.multiple_of(p * piece, piece), piece)
        return pltpu.make_async_remote_copy(
            src_ref=part_out.at[dest, span],
            dst_ref=blocks.at[k, span],
            send_sem=part_send.at[p, k],
            recv_sem=part_recv.at[p, k],
            device_id=(dest, col),
            device_id_type=MESH_ID,
        )

    def start_part(i, carry):
        part_copy(lax.rem(i, n - 1) + 1, i // (n - 1)).start()
        return carry

    lax.fori_loop(0, (n - 1) * pieces, start_part, 0)
    total[...] = part_out[me].astype(jnp.float32)

    def add_block(k, carry):
        for p in range(pieces):
            part_copy(k, p).wait()
        total[...] += blocks[k].astype(jnp.float32)
        return carry

    lax.fori_loop(1, n, add_block, 0)
    new_first, new_second, direction = adam_moments(total[...], first_ref[...], second_ref[...])
    new_first_ref[...] = new_first
    new_second_ref[...] = new_second
    direction_ref[...] = direction

    update[...] = (
        lax.dot_general(
            proj_ref[...],
            direction_ref[...],
            (((1,), (1,)), ((), ())),
            preferred_element_type=jnp.float32,
        )
        .astype(jnp.bfloat16)
        .reshape(update.shape)
    )
    local = pltpu.make_async_copy(update, sendbuf, local_sem)
    local.start()
    local.wait()
    copies = []
    for k in range(1, n):
        dest = lax.rem(me + k, n)
        copy = pltpu.make_async_remote_copy(
            src_ref=sendbuf.at[dest],
            dst_ref=recv.at[k],
            send_sem=send_sem.at[k],
            recv_sem=recv_sem.at[k],
            device_id=(dest, col),
            device_id_type=MESH_ID,
        )
        copy.start()
        copies.append(copy)

    def apply(source, block):
        cols = pl.ds(pl.multiple_of(source * width, width), width)
        new_weight_ref[:, cols] = (
            weight_ref[:, cols].astype(jnp.float32) - step_rate * block.astype(jnp.float32)
        ).astype(jnp.bfloat16)

    apply(me, sendbuf[me])
    for k, copy in enumerate(copies, 1):
        copy.wait()
        apply(lax.rem(me + n - k, n), recv[k])


def step(out_grad, proj_hi, proj_lo, first_moment, second_moment, projector, weight, n):
    pieces = 8
    hidden = out_grad.shape[1] // n
    rank = proj_hi.shape[1]
    rows = weight.shape[0]
    vmem = pl.BlockSpec(memory_space=pltpu.VMEM)
    return pl.pallas_call(
        functools.partial(step_kernel, n, pieces),
        out_shape=(
            jax.ShapeDtypeStruct(weight.shape, weight.dtype),
            jax.ShapeDtypeStruct((hidden, rank), jnp.float32),
            jax.ShapeDtypeStruct((hidden, rank), jnp.float32),
        ),
        in_specs=[vmem] * 7,
        out_specs=(vmem, vmem, vmem),
        scratch_shapes=[
            pltpu.VMEM((n, hidden, rank), jnp.bfloat16),
            pltpu.VMEM((n, hidden, rank), jnp.bfloat16),
            pltpu.VMEM((n, hidden, rank), jnp.bfloat16),
            pltpu.VMEM((hidden, rank), jnp.float32),
            pltpu.VMEM((hidden, rank), jnp.bfloat16),
            pltpu.VMEM((n, rows, hidden), jnp.bfloat16),
            pltpu.VMEM((n, rows, hidden), jnp.bfloat16),
            pltpu.VMEM((n, rows, hidden), jnp.bfloat16),
            pltpu.SemaphoreType.DMA(()),
            pltpu.SemaphoreType.DMA((pieces, n)),
            pltpu.SemaphoreType.DMA((pieces, n)),
            pltpu.SemaphoreType.DMA((n,)),
            pltpu.SemaphoreType.DMA((n,)),
        ],
        compiler_params=pltpu.CompilerParams(
            collective_id=2, has_side_effects=True, vmem_limit_bytes=64 * 1024 * 1024
        ),
    )(out_grad, proj_hi, proj_lo, first_moment, second_moment, projector, weight)


def chip_gather_kernel(
    acts_ref, proj_ref, hi_ref, lo_ref, q_buf, send_buf, recv, local_sem, send_sem, recv_sem
):
    me = lax.axis_index("tensor")
    core_peer = me + 1 - 2 * lax.rem(me, 2)
    chip_peer = lax.rem(me + 2, 4)
    barrier = pltpu.get_barrier_semaphore()
    for peer in (core_peer, chip_peer):
        pl.semaphore_signal(barrier, inc=1, device_id={"tensor": peer}, device_id_type=MESH_ID)
    q_buf[...] = jnp.dot(acts_ref[...], proj_ref[...], preferred_element_type=jnp.float32)
    local = pltpu.make_async_copy(q_buf, send_buf, local_sem)
    local.start()
    local.wait()
    pl.semaphore_wait(barrier, 2)

    def send(src, slot, peer):
        copy = pltpu.make_async_remote_copy(
            src_ref=src,
            dst_ref=recv.at[slot],
            send_sem=send_sem.at[slot],
            recv_sem=recv_sem.at[slot],
            device_id={"tensor": peer},
            device_id_type=MESH_ID,
        )
        copy.start()
        return copy

    def split(slot, piece):
        hi = piece.astype(jnp.bfloat16)
        hi_ref[slot] = hi
        lo_ref[slot] = (piece - hi.astype(jnp.float32)).astype(jnp.bfloat16)

    across = send(send_buf, 1, chip_peer)
    beside = send(send_buf, 0, core_peer)
    split(me, send_buf[...])
    across.wait()
    forward = send(recv.at[1], 2, core_peer)
    split(chip_peer, recv[1])
    beside.wait()
    split(core_peer, recv[0])
    forward.wait()
    split(3 - me, recv[2])


def chip_gather(acts, projector):
    shape = (acts.shape[0], projector.shape[1])
    vmem = pl.BlockSpec(memory_space=pltpu.VMEM)
    return pl.pallas_call(
        chip_gather_kernel,
        out_shape=(
            jax.ShapeDtypeStruct((4,) + shape, jnp.bfloat16),
            jax.ShapeDtypeStruct((4,) + shape, jnp.bfloat16),
        ),
        in_specs=[vmem, vmem],
        out_specs=(vmem, vmem),
        scratch_shapes=[
            pltpu.VMEM(shape, jnp.float32),
            pltpu.VMEM(shape, jnp.float32),
            pltpu.VMEM((3,) + shape, jnp.float32),
            pltpu.SemaphoreType.DMA(()),
            pltpu.SemaphoreType.DMA((3,)),
            pltpu.SemaphoreType.DMA((3,)),
        ],
        compiler_params=pltpu.CompilerParams(
            collective_id=1, has_side_effects=True, vmem_limit_bytes=48 * 1024 * 1024
        ),
    )(acts, projector)


def per_device(acts, out_grad, projector, weight, first_moment, second_moment):
    assert lax.axis_size("tensor") == 4
    proj_hi, proj_lo = chip_gather(acts, projector)
    proj_hi = proj_hi.reshape(-1, proj_hi.shape[2])
    proj_lo = proj_lo.reshape(-1, proj_lo.shape[2])
    new_weight, new_first, new_second = step(
        out_grad, proj_hi, proj_lo, first_moment[0], second_moment[0], projector, weight,
        lax.axis_size("dp"),
    )
    return (new_weight, new_first[None], new_second[None])


def solution(mesh):
    return jax.shard_map(
        per_device,
        mesh=mesh,
        in_specs=(
            P(("dp", "tensor"), None),
            P("dp", "tensor"),
            P(),
            P("dp", "tensor"),
            P("tensor", "dp", None),
            P("tensor", "dp", None),
        ),
        out_specs=(P("dp", "tensor"), P("tensor", "dp", None), P("tensor", "dp", None)),
        check_vma=False,
    )
```

```python
import functools

import jax
import jax.numpy as jnp
from jax import lax
from jax.experimental import pallas as pl
from jax.experimental.pallas import tpu as pltpu
from jax.sharding import PartitionSpec as P

beta_first = 0.9
beta_second = 0.95
adam_step = 10
epsilon = 1e-08
step_rate = 0.5

MESH_ID = pl.DeviceIdType.MESH


def adam_moments(lowgrad, first_moment, second_moment):
    new_first = beta_first * first_moment + (1.0 - beta_first) * lowgrad
    new_second = beta_second * second_moment + (1.0 - beta_second) * lowgrad * lowgrad
    corrected_first = new_first / (1.0 - beta_first**adam_step)
    corrected_second = new_second / (1.0 - beta_second**adam_step)
    direction = (corrected_first / (jnp.sqrt(corrected_second) + epsilon)).astype(jnp.bfloat16)
    return (new_first, new_second, direction)


def tail_kernel(
    n, pieces, blocks_ref, first_ref, second_ref, proj_ref, weight_ref,
    new_weight_ref, new_first_ref, new_second_ref,
    total, direction_ref, update, sendbuf, recv, local_sem, send_sem, recv_sem,
):
    me = lax.axis_index("dp")
    col = lax.axis_index("tensor")
    rows = sendbuf.shape[1]
    width = sendbuf.shape[2]
    barrier = pltpu.get_barrier_semaphore()
    for k in range(1, n):
        pl.semaphore_signal(
            barrier, inc=1, device_id=(lax.rem(me + k, n), col), device_id_type=MESH_ID
        )

    total[...] = blocks_ref[0].astype(jnp.float32)

    def add_block(k, carry):
        total[...] += blocks_ref[k].astype(jnp.float32)
        return carry

    lax.fori_loop(1, n, add_block, 0)
    new_first, new_second, direction = adam_moments(total[...], first_ref[...], second_ref[...])
    new_first_ref[...] = new_first
    new_second_ref[...] = new_second
    direction_ref[...] = direction

    update[...] = (
        lax.dot_general(
            proj_ref[...],
            direction_ref[...],
            (((1,), (1,)), ((), ())),
            preferred_element_type=jnp.float32,
        )
        .astype(jnp.bfloat16)
        .reshape(update.shape)
    )
    local = pltpu.make_async_copy(update, sendbuf, local_sem)
    local.start()
    local.wait()
    pl.semaphore_wait(barrier, n - 1)
    piece = rows // pieces

    def block_copy(k, p):
        dest = lax.rem(me + k, n)
        span = pl.ds(pl.multiple_of(p * piece, piece), piece)
        return pltpu.make_async_remote_copy(
            src_ref=sendbuf.at[dest, span],
            dst_ref=recv.at[k, span],
            send_sem=send_sem.at[p, k],
            recv_sem=recv_sem.at[p, k],
            device_id=(dest, col),
            device_id_type=MESH_ID,
        )

    def start_block(i, carry):
        block_copy(lax.rem(i, n - 1) + 1, i // (n - 1)).start()
        return carry

    lax.fori_loop(0, (n - 1) * pieces, start_block, 0)

    def apply(source, block):
        cols = pl.ds(pl.multiple_of(source * width, width), width)
        new_weight_ref[:, cols] = (
            weight_ref[:, cols].astype(jnp.float32) - step_rate * block.astype(jnp.float32)
        ).astype(jnp.bfloat16)

    apply(me, sendbuf[me])

    def land(k, carry):
        for p in range(pieces):
            block_copy(k, p).wait()
        apply(lax.rem(me + n - k, n), recv[k])
        return carry

    lax.fori_loop(1, n, land, 0)


def tail(blocks, first_moment, second_moment, projector, weight):
    n, hidden, rank = blocks.shape
    rows = weight.shape[0]
    vmem = pl.BlockSpec(memory_space=pltpu.VMEM)
    return pl.pallas_call(
        functools.partial(tail_kernel, n, 4),
        out_shape=(
            jax.ShapeDtypeStruct(weight.shape, weight.dtype),
            jax.ShapeDtypeStruct((hidden, rank), jnp.float32),
            jax.ShapeDtypeStruct((hidden, rank), jnp.float32),
        ),
        in_specs=[vmem] * 5,
        out_specs=(vmem, vmem, vmem),
        scratch_shapes=[
            pltpu.VMEM((hidden, rank), jnp.float32),
            pltpu.VMEM((hidden, rank), jnp.bfloat16),
            pltpu.VMEM((n, rows, hidden), jnp.bfloat16),
            pltpu.VMEM((n, rows, hidden), jnp.bfloat16),
            pltpu.VMEM((n, rows, hidden), jnp.bfloat16),
            pltpu.SemaphoreType.DMA(()),
            pltpu.SemaphoreType.DMA((4, n)),
            pltpu.SemaphoreType.DMA((4, n)),
        ],
        compiler_params=pltpu.CompilerParams(
            collective_id=2, has_side_effects=True, vmem_limit_bytes=48 * 1024 * 1024
        ),
    )(blocks, first_moment, second_moment, projector, weight)


def chip_gather_kernel(
    acts_ref, proj_ref, hi_ref, lo_ref, q_buf, send_buf, recv, local_sem, send_sem, recv_sem
):
    me = lax.axis_index("tensor")
    core_peer = me + 1 - 2 * lax.rem(me, 2)
    chip_peer = lax.rem(me + 2, 4)
    barrier = pltpu.get_barrier_semaphore()
    for peer in (core_peer, chip_peer):
        pl.semaphore_signal(barrier, inc=1, device_id={"tensor": peer}, device_id_type=MESH_ID)
    q_buf[...] = jnp.dot(acts_ref[...], proj_ref[...], preferred_element_type=jnp.float32)
    local = pltpu.make_async_copy(q_buf, send_buf, local_sem)
    local.start()
    local.wait()
    pl.semaphore_wait(barrier, 2)

    def send(src, slot, peer):
        copy = pltpu.make_async_remote_copy(
            src_ref=src,
            dst_ref=recv.at[slot],
            send_sem=send_sem.at[slot],
            recv_sem=recv_sem.at[slot],
            device_id={"tensor": peer},
            device_id_type=MESH_ID,
        )
        copy.start()
        return copy

    def split(slot, piece):
        hi = piece.astype(jnp.bfloat16)
        hi_ref[slot] = hi
        lo_ref[slot] = (piece - hi.astype(jnp.float32)).astype(jnp.bfloat16)

    across = send(send_buf, 1, chip_peer)
    beside = send(send_buf, 0, core_peer)
    split(me, send_buf[...])
    across.wait()
    forward = send(recv.at[1], 2, core_peer)
    split(chip_peer, recv[1])
    beside.wait()
    split(core_peer, recv[0])
    forward.wait()
    split(3 - me, recv[2])


def chip_gather(acts, projector):
    shape = (acts.shape[0], projector.shape[1])
    vmem = pl.BlockSpec(memory_space=pltpu.VMEM)
    return pl.pallas_call(
        chip_gather_kernel,
        out_shape=(
            jax.ShapeDtypeStruct((4,) + shape, jnp.bfloat16),
            jax.ShapeDtypeStruct((4,) + shape, jnp.bfloat16),
        ),
        in_specs=[vmem, vmem],
        out_specs=(vmem, vmem),
        scratch_shapes=[
            pltpu.VMEM(shape, jnp.float32),
            pltpu.VMEM(shape, jnp.float32),
            pltpu.VMEM((3,) + shape, jnp.float32),
            pltpu.SemaphoreType.DMA(()),
            pltpu.SemaphoreType.DMA((3,)),
            pltpu.SemaphoreType.DMA((3,)),
        ],
        compiler_params=pltpu.CompilerParams(
            collective_id=1, has_side_effects=True, vmem_limit_bytes=48 * 1024 * 1024
        ),
    )(acts, projector)


def per_device(acts, out_grad, projector, weight, first_moment, second_moment):
    assert lax.axis_size("tensor") == 4
    proj_hi, proj_lo = chip_gather(acts, projector)
    proj_hi = proj_hi.reshape(-1, proj_hi.shape[2])
    proj_lo = proj_lo.reshape(-1, proj_lo.shape[2])
    owners = lax.axis_size("dp")
    grad_blocks = out_grad.reshape(out_grad.shape[0], owners, -1)
    dims = (((0,), (0,)), ((), ()))
    partial = lax.dot_general(
        grad_blocks, proj_hi, dims, preferred_element_type=jnp.float32
    ) + lax.dot_general(grad_blocks, proj_lo, dims, preferred_element_type=jnp.float32)
    blocks = lax.all_to_all(
        partial.astype(jnp.bfloat16), "dp", split_axis=0, concat_axis=0, tiled=True
    )
    new_weight, new_first, new_second = tail(
        blocks, first_moment[0], second_moment[0], projector, weight
    )
    return (new_weight, new_first[None], new_second[None])


def solution(mesh):
    return jax.shard_map(
        per_device,
        mesh=mesh,
        in_specs=(
            P(("dp", "tensor"), None),
            P("dp", "tensor"),
            P(),
            P("dp", "tensor"),
            P("tensor", "dp", None),
            P("tensor", "dp", None),
        ),
        out_specs=(P("dp", "tensor"), P("tensor", "dp", None), P("tensor", "dp", None)),
        check_vma=False,
    )
```

```python
import functools

import jax
import jax.numpy as jnp
from jax import lax
from jax.experimental import pallas as pl
from jax.experimental.pallas import tpu as pltpu
from jax.sharding import PartitionSpec as P

beta_first = 0.9
beta_second = 0.95
adam_step = 10
epsilon = 1e-08
step_rate = 0.5

MESH_ID = pl.DeviceIdType.MESH


def adam_moments(lowgrad, first_moment, second_moment):
    new_first = beta_first * first_moment + (1.0 - beta_first) * lowgrad
    new_second = beta_second * second_moment + (1.0 - beta_second) * lowgrad * lowgrad
    corrected_first = new_first / (1.0 - beta_first**adam_step)
    corrected_second = new_second / (1.0 - beta_second**adam_step)
    direction = (corrected_first / (jnp.sqrt(corrected_second) + epsilon)).astype(jnp.bfloat16)
    return (new_first, new_second, direction)


def tail_kernel(
    n, blocks_ref, first_ref, second_ref, proj_ref, weight_ref,
    new_weight_ref, new_first_ref, new_second_ref,
    total, direction_ref, update, sendbuf, recv, local_sem, send_sem, recv_sem,
):
    me = lax.axis_index("dp")
    col = lax.axis_index("tensor")
    rows = sendbuf.shape[1]
    width = sendbuf.shape[2]
    barrier = pltpu.get_barrier_semaphore()
    for k in range(1, n):
        pl.semaphore_signal(
            barrier, inc=1, device_id=(lax.rem(me + k, n), col), device_id_type=MESH_ID
        )

    band = 16

    def rows_step(r, carry):
        rs = pl.ds(pl.multiple_of(r * band, band), band)
        lowgrad = blocks_ref[0, rs, :].astype(jnp.float32)
        for k in range(1, n):
            lowgrad += blocks_ref[k, rs, :].astype(jnp.float32)
        new_first, new_second, direction = adam_moments(
            lowgrad, first_ref[rs, :], second_ref[rs, :]
        )
        new_first_ref[rs, :] = new_first
        new_second_ref[rs, :] = new_second
        direction_ref[rs, :] = direction
        return carry

    lax.fori_loop(0, blocks_ref.shape[1] // band, rows_step, 0)

    update[...] = (
        lax.dot_general(
            proj_ref[...],
            direction_ref[...],
            (((1,), (1,)), ((), ())),
            preferred_element_type=jnp.float32,
        )
        .astype(jnp.bfloat16)
        .reshape(update.shape)
    )
    local = pltpu.make_async_copy(update, sendbuf, local_sem)
    local.start()
    local.wait()
    pl.semaphore_wait(barrier, n - 1)
    copies = []
    for k in range(1, n):
        dest = lax.rem(me + k, n)
        copy = pltpu.make_async_remote_copy(
            src_ref=sendbuf.at[dest],
            dst_ref=recv.at[k],
            send_sem=send_sem.at[k],
            recv_sem=recv_sem.at[k],
            device_id=(dest, col),
            device_id_type=MESH_ID,
        )
        copy.start()
        copies.append(copy)

    def apply(source, block):
        cols = pl.ds(pl.multiple_of(source * width, width), width)
        new_weight_ref[:, cols] = (
            weight_ref[:, cols].astype(jnp.float32) - step_rate * block.astype(jnp.float32)
        ).astype(jnp.bfloat16)

    apply(me, sendbuf[me])
    for k, copy in enumerate(copies, 1):
        copy.wait()
        apply(lax.rem(me + n - k, n), recv[k])


def tail(blocks, first_moment, second_moment, projector, weight):
    n, hidden, rank = blocks.shape
    rows = weight.shape[0]
    vmem = pl.BlockSpec(memory_space=pltpu.VMEM)
    return pl.pallas_call(
        functools.partial(tail_kernel, n),
        out_shape=(
            jax.ShapeDtypeStruct(weight.shape, weight.dtype),
            jax.ShapeDtypeStruct((hidden, rank), jnp.float32),
            jax.ShapeDtypeStruct((hidden, rank), jnp.float32),
        ),
        in_specs=[vmem] * 5,
        out_specs=(vmem, vmem, vmem),
        scratch_shapes=[
            pltpu.VMEM((hidden, rank), jnp.float32),
            pltpu.VMEM((hidden, rank), jnp.bfloat16),
            pltpu.VMEM((n, rows, hidden), jnp.bfloat16),
            pltpu.VMEM((n, rows, hidden), jnp.bfloat16),
            pltpu.VMEM((n, rows, hidden), jnp.bfloat16),
            pltpu.SemaphoreType.DMA(()),
            pltpu.SemaphoreType.DMA((n,)),
            pltpu.SemaphoreType.DMA((n,)),
        ],
        compiler_params=pltpu.CompilerParams(
            collective_id=2, has_side_effects=True, vmem_limit_bytes=48 * 1024 * 1024
        ),
    )(blocks, first_moment, second_moment, projector, weight)


def chip_gather_kernel(
    acts_ref, proj_ref, hi_ref, lo_ref, q_buf, send_buf, recv, local_sem, send_sem, recv_sem
):
    me = lax.axis_index("tensor")
    core_peer = me + 1 - 2 * lax.rem(me, 2)
    chip_peer = lax.rem(me + 2, 4)
    barrier = pltpu.get_barrier_semaphore()
    for peer in (core_peer, chip_peer):
        pl.semaphore_signal(barrier, inc=1, device_id={"tensor": peer}, device_id_type=MESH_ID)
    q_buf[...] = jnp.dot(acts_ref[...], proj_ref[...], preferred_element_type=jnp.float32)
    local = pltpu.make_async_copy(q_buf, send_buf, local_sem)
    local.start()
    local.wait()
    pl.semaphore_wait(barrier, 2)

    def send(src, slot, peer):
        copy = pltpu.make_async_remote_copy(
            src_ref=src,
            dst_ref=recv.at[slot],
            send_sem=send_sem.at[slot],
            recv_sem=recv_sem.at[slot],
            device_id={"tensor": peer},
            device_id_type=MESH_ID,
        )
        copy.start()
        return copy

    def split(slot, piece):
        hi = piece.astype(jnp.bfloat16)
        hi_ref[slot] = hi
        lo_ref[slot] = (piece - hi.astype(jnp.float32)).astype(jnp.bfloat16)

    across = send(send_buf, 1, chip_peer)
    beside = send(send_buf, 0, core_peer)
    split(me, send_buf[...])
    across.wait()
    forward = send(recv.at[1], 2, core_peer)
    split(chip_peer, recv[1])
    beside.wait()
    split(core_peer, recv[0])
    forward.wait()
    split(3 - me, recv[2])


def chip_gather(acts, projector):
    shape = (acts.shape[0], projector.shape[1])
    vmem = pl.BlockSpec(memory_space=pltpu.VMEM)
    return pl.pallas_call(
        chip_gather_kernel,
        out_shape=(
            jax.ShapeDtypeStruct((4,) + shape, jnp.bfloat16),
            jax.ShapeDtypeStruct((4,) + shape, jnp.bfloat16),
        ),
        in_specs=[vmem, vmem],
        out_specs=(vmem, vmem),
        scratch_shapes=[
            pltpu.VMEM(shape, jnp.float32),
            pltpu.VMEM(shape, jnp.float32),
            pltpu.VMEM((3,) + shape, jnp.float32),
            pltpu.SemaphoreType.DMA(()),
            pltpu.SemaphoreType.DMA((3,)),
            pltpu.SemaphoreType.DMA((3,)),
        ],
        compiler_params=pltpu.CompilerParams(
            collective_id=1, has_side_effects=True, vmem_limit_bytes=48 * 1024 * 1024
        ),
    )(acts, projector)


def per_device(acts, out_grad, projector, weight, first_moment, second_moment):
    assert lax.axis_size("tensor") == 4
    proj_hi, proj_lo = chip_gather(acts, projector)
    proj_hi = proj_hi.reshape(-1, proj_hi.shape[2])
    proj_lo = proj_lo.reshape(-1, proj_lo.shape[2])
    owners = lax.axis_size("dp")
    grad_blocks = out_grad.reshape(out_grad.shape[0], owners, -1)
    dims = (((0,), (0,)), ((), ()))
    partial = lax.dot_general(
        grad_blocks, proj_hi, dims, preferred_element_type=jnp.float32
    ) + lax.dot_general(grad_blocks, proj_lo, dims, preferred_element_type=jnp.float32)
    blocks = lax.all_to_all(
        partial.astype(jnp.bfloat16), "dp", split_axis=0, concat_axis=0, tiled=True
    )
    new_weight, new_first, new_second = tail(
        blocks, first_moment[0], second_moment[0], projector, weight
    )
    return (new_weight, new_first[None], new_second[None])


def solution(mesh):
    return jax.shard_map(
        per_device,
        mesh=mesh,
        in_specs=(
            P(("dp", "tensor"), None),
            P("dp", "tensor"),
            P(),
            P("dp", "tensor"),
            P("tensor", "dp", None),
            P("tensor", "dp", None),
        ),
        out_specs=(P("dp", "tensor"), P("tensor", "dp", None), P("tensor", "dp", None)),
        check_vma=False,
    )
```

```python
import functools

import jax
import jax.numpy as jnp
from jax import lax
from jax.experimental import pallas as pl
from jax.experimental.pallas import tpu as pltpu
from jax.sharding import PartitionSpec as P

beta_first = 0.9
beta_second = 0.95
adam_step = 10
epsilon = 1e-08
step_rate = 0.5

MESH_ID = pl.DeviceIdType.MESH


def adam_moments(lowgrad, first_moment, second_moment):
    new_first = beta_first * first_moment + (1.0 - beta_first) * lowgrad
    new_second = beta_second * second_moment + (1.0 - beta_second) * lowgrad * lowgrad
    corrected_first = new_first / (1.0 - beta_first**adam_step)
    corrected_second = new_second / (1.0 - beta_second**adam_step)
    direction = (corrected_first / (jnp.sqrt(corrected_second) + epsilon)).astype(jnp.bfloat16)
    return (new_first, new_second, direction)


def tail_kernel(
    n, blocks_ref, first_ref, second_ref, proj_ref, weight_ref,
    new_weight_ref, new_first_ref, new_second_ref,
    total, direction_ref, update, sendbuf, recv, local_sem, send_sem, recv_sem,
):
    me = lax.axis_index("dp")
    col = lax.axis_index("tensor")
    rows = sendbuf.shape[1]
    width = sendbuf.shape[2]
    barrier = pltpu.get_barrier_semaphore()
    for k in range(1, n):
        pl.semaphore_signal(
            barrier, inc=1, device_id=(lax.rem(me + k, n), col), device_id_type=MESH_ID
        )

    band = 16

    def rows_step(r, carry):
        rs = pl.ds(pl.multiple_of(r * band, band), band)
        lowgrad = blocks_ref[0, rs, :].astype(jnp.float32)
        for k in range(1, n):
            lowgrad += blocks_ref[k, rs, :].astype(jnp.float32)
        new_first, new_second, direction = adam_moments(
            lowgrad, first_ref[rs, :], second_ref[rs, :]
        )
        new_first_ref[rs, :] = new_first
        new_second_ref[rs, :] = new_second
        direction_ref[rs, :] = direction
        return carry

    lax.fori_loop(0, blocks_ref.shape[1] // band, rows_step, 0)

    update[...] = (
        lax.dot_general(
            proj_ref[...],
            direction_ref[...],
            (((1,), (1,)), ((), ())),
            preferred_element_type=jnp.float32,
        )
        .astype(jnp.bfloat16)
        .reshape(update.shape)
    )
    local = pltpu.make_async_copy(update, sendbuf, local_sem)
    local.start()
    local.wait()
    pl.semaphore_wait(barrier, n - 1)
    copies = []
    for k in range(1, n):
        dest = lax.rem(me + k, n)
        copy = pltpu.make_async_remote_copy(
            src_ref=sendbuf.at[dest],
            dst_ref=recv.at[k],
            send_sem=send_sem.at[k],
            recv_sem=recv_sem.at[k],
            device_id=(dest, col),
            device_id_type=MESH_ID,
        )
        copy.start()
        copies.append(copy)

    def apply(source, block):
        cols = pl.ds(pl.multiple_of(source * width, width), width)
        new_weight_ref[:, cols] = (
            weight_ref[:, cols].astype(jnp.float32) - step_rate * block.astype(jnp.float32)
        ).astype(jnp.bfloat16)

    apply(me, sendbuf[me])
    for k, copy in enumerate(copies, 1):
        copy.wait()
        apply(lax.rem(me + n - k, n), recv[k])


def tail(blocks, first_moment, second_moment, projector, weight):
    n, hidden, rank = blocks.shape
    rows = weight.shape[0]
    vmem = pl.BlockSpec(memory_space=pltpu.VMEM)
    return pl.pallas_call(
        functools.partial(tail_kernel, n),
        out_shape=(
            jax.ShapeDtypeStruct(weight.shape, weight.dtype),
            jax.ShapeDtypeStruct((hidden, rank), jnp.float32),
            jax.ShapeDtypeStruct((hidden, rank), jnp.float32),
        ),
        in_specs=[vmem] * 5,
        out_specs=(vmem, vmem, vmem),
        scratch_shapes=[
            pltpu.VMEM((hidden, rank), jnp.float32),
            pltpu.VMEM((hidden, rank), jnp.bfloat16),
            pltpu.VMEM((n, rows, hidden), jnp.bfloat16),
            pltpu.VMEM((n, rows, hidden), jnp.bfloat16),
            pltpu.VMEM((n, rows, hidden), jnp.bfloat16),
            pltpu.SemaphoreType.DMA(()),
            pltpu.SemaphoreType.DMA((n,)),
            pltpu.SemaphoreType.DMA((n,)),
        ],
        compiler_params=pltpu.CompilerParams(
            collective_id=2, has_side_effects=True, vmem_limit_bytes=48 * 1024 * 1024
        ),
    )(blocks, first_moment, second_moment, projector, weight)


def chip_gather_kernel(
    acts_ref, proj_ref, hi_ref, lo_ref, q_buf, send_buf, recv, local_sem, send_sem, recv_sem
):
    me = lax.axis_index("tensor")
    core_peer = me + 1 - 2 * lax.rem(me, 2)
    chip_peer = lax.rem(me + 2, 4)
    barrier = pltpu.get_barrier_semaphore()
    for peer in (core_peer, chip_peer):
        pl.semaphore_signal(barrier, inc=1, device_id={"tensor": peer}, device_id_type=MESH_ID)
    q_buf[...] = jnp.dot(acts_ref[...], proj_ref[...], preferred_element_type=jnp.float32)
    local = pltpu.make_async_copy(q_buf, send_buf, local_sem)
    local.start()
    local.wait()
    pl.semaphore_wait(barrier, 2)

    half = send_buf.shape[0] // 2

    def send(src, slot, peer, p):
        span = pl.ds(p * half, half)
        copy = pltpu.make_async_remote_copy(
            src_ref=src.at[span],
            dst_ref=recv.at[slot, span],
            send_sem=send_sem.at[slot, p],
            recv_sem=recv_sem.at[slot, p],
            device_id={"tensor": peer},
            device_id_type=MESH_ID,
        )
        copy.start()
        return copy

    def split(slot, piece):
        hi = piece.astype(jnp.bfloat16)
        hi_ref[slot] = hi
        lo_ref[slot] = (piece - hi.astype(jnp.float32)).astype(jnp.bfloat16)

    across = [send(send_buf, 1, chip_peer, p) for p in range(2)]
    beside = [send(send_buf, 0, core_peer, p) for p in range(2)]
    split(me, send_buf[...])
    forward = []
    for p in range(2):
        across[p].wait()
        forward.append(send(recv.at[1], 2, core_peer, p))
    split(chip_peer, recv[1])
    for copy in beside:
        copy.wait()
    split(core_peer, recv[0])
    for copy in forward:
        copy.wait()
    split(3 - me, recv[2])


def chip_gather(acts, projector):
    shape = (acts.shape[0], projector.shape[1])
    vmem = pl.BlockSpec(memory_space=pltpu.VMEM)
    return pl.pallas_call(
        chip_gather_kernel,
        out_shape=(
            jax.ShapeDtypeStruct((4,) + shape, jnp.bfloat16),
            jax.ShapeDtypeStruct((4,) + shape, jnp.bfloat16),
        ),
        in_specs=[vmem, vmem],
        out_specs=(vmem, vmem),
        scratch_shapes=[
            pltpu.VMEM(shape, jnp.float32),
            pltpu.VMEM(shape, jnp.float32),
            pltpu.VMEM((3,) + shape, jnp.float32),
            pltpu.SemaphoreType.DMA(()),
            pltpu.SemaphoreType.DMA((3, 2)),
            pltpu.SemaphoreType.DMA((3, 2)),
        ],
        compiler_params=pltpu.CompilerParams(
            collective_id=1, has_side_effects=True, vmem_limit_bytes=48 * 1024 * 1024
        ),
    )(acts, projector)


def per_device(acts, out_grad, projector, weight, first_moment, second_moment):
    assert lax.axis_size("tensor") == 4
    proj_hi, proj_lo = chip_gather(acts, projector)
    proj_hi = proj_hi.reshape(-1, proj_hi.shape[2])
    proj_lo = proj_lo.reshape(-1, proj_lo.shape[2])
    owners = lax.axis_size("dp")
    grad_blocks = out_grad.reshape(out_grad.shape[0], owners, -1)
    dims = (((0,), (0,)), ((), ()))
    partial = lax.dot_general(
        grad_blocks, proj_hi, dims, preferred_element_type=jnp.float32
    ) + lax.dot_general(grad_blocks, proj_lo, dims, preferred_element_type=jnp.float32)
    blocks = lax.all_to_all(
        partial.astype(jnp.bfloat16), "dp", split_axis=0, concat_axis=0, tiled=True
    )
    new_weight, new_first, new_second = tail(
        blocks, first_moment[0], second_moment[0], projector, weight
    )
    return (new_weight, new_first[None], new_second[None])


def solution(mesh):
    return jax.shard_map(
        per_device,
        mesh=mesh,
        in_specs=(
            P(("dp", "tensor"), None),
            P("dp", "tensor"),
            P(),
            P("dp", "tensor"),
            P("tensor", "dp", None),
            P("tensor", "dp", None),
        ),
        out_specs=(P("dp", "tensor"), P("tensor", "dp", None), P("tensor", "dp", None)),
        check_vma=False,
    )
```

```python
import functools

import jax
import jax.numpy as jnp
from jax import lax
from jax.experimental import pallas as pl
from jax.experimental.pallas import tpu as pltpu
from jax.sharding import PartitionSpec as P

beta_first = 0.9
beta_second = 0.95
adam_step = 10
epsilon = 1e-08
step_rate = 0.5

MESH_ID = pl.DeviceIdType.MESH


def adam_moments(lowgrad, first_moment, second_moment):
    new_first = beta_first * first_moment + (1.0 - beta_first) * lowgrad
    new_second = beta_second * second_moment + (1.0 - beta_second) * lowgrad * lowgrad
    corrected_first = new_first / (1.0 - beta_first**adam_step)
    corrected_second = new_second / (1.0 - beta_second**adam_step)
    direction = (corrected_first / (jnp.sqrt(corrected_second) + epsilon)).astype(jnp.bfloat16)
    return (new_first, new_second, direction)


def step_kernel(
    n, pieces, grad_ref, hi_ref, lo_ref, first_ref, second_ref, proj_ref, weight_ref,
    new_weight_ref, new_first_ref, new_second_ref,
    part, part_out, blocks, total, hi_t, lo_t, direction_ref, update, sendbuf, recv,
    local_sem, part_send, part_recv, send_sem, recv_sem,
):
    me = lax.axis_index("dp")
    col = lax.axis_index("tensor")
    owned = part.shape[2]
    rows = sendbuf.shape[1]
    width = sendbuf.shape[2]
    barrier = pltpu.get_barrier_semaphore()
    for k in range(1, n):
        pl.semaphore_signal(
            barrier, inc=1, device_id=(lax.rem(me + k, n), col), device_id_type=MESH_ID
        )

    hi_t[...] = hi_ref[...].T
    lo_t[...] = lo_ref[...].T

    def partial_block(j, carry):
        grad = grad_ref[:, pl.ds(pl.multiple_of(j * owned, owned), owned)]
        term = jnp.dot(hi_t[...], grad, preferred_element_type=jnp.float32)
        term += jnp.dot(lo_t[...], grad, preferred_element_type=jnp.float32)
        part[j] = term.astype(jnp.bfloat16)
        return carry

    lax.fori_loop(0, n, partial_block, 0)
    local = pltpu.make_async_copy(part, part_out, local_sem)
    local.start()
    local.wait()
    pl.semaphore_wait(barrier, n - 1)
    piece = part.shape[1] // pieces

    def part_copy(k, p):
        dest = lax.rem(me + k, n)
        span = pl.ds(pl.multiple_of(p * piece, piece), piece)
        return pltpu.make_async_remote_copy(
            src_ref=part_out.at[dest, span],
            dst_ref=blocks.at[k, span],
            send_sem=part_send.at[p, k],
            recv_sem=part_recv.at[p, k],
            device_id=(dest, col),
            device_id_type=MESH_ID,
        )

    def start_part(i, carry):
        part_copy(lax.rem(i, n - 1) + 1, i // (n - 1)).start()
        return carry

    lax.fori_loop(0, (n - 1) * pieces, start_part, 0)
    total[...] = part_out[me].astype(jnp.float32)

    def add_block(k, carry):
        for p in range(pieces):
            part_copy(k, p).wait()
        total[...] += blocks[k].astype(jnp.float32)
        return carry

    lax.fori_loop(1, n, add_block, 0)
    new_first, new_second, direction = adam_moments(total[...].T, first_ref[...], second_ref[...])
    new_first_ref[...] = new_first
    new_second_ref[...] = new_second
    direction_ref[...] = direction

    update[...] = (
        lax.dot_general(
            proj_ref[...],
            direction_ref[...],
            (((1,), (1,)), ((), ())),
            preferred_element_type=jnp.float32,
        )
        .astype(jnp.bfloat16)
        .reshape(update.shape)
    )
    local = pltpu.make_async_copy(update, sendbuf, local_sem)
    local.start()
    local.wait()
    copies = []
    for k in range(1, n):
        dest = lax.rem(me + k, n)
        copy = pltpu.make_async_remote_copy(
            src_ref=sendbuf.at[dest],
            dst_ref=recv.at[k],
            send_sem=send_sem.at[k],
            recv_sem=recv_sem.at[k],
            device_id=(dest, col),
            device_id_type=MESH_ID,
        )
        copy.start()
        copies.append(copy)

    def apply(source, block):
        cols = pl.ds(pl.multiple_of(source * width, width), width)
        new_weight_ref[:, cols] = (
            weight_ref[:, cols].astype(jnp.float32) - step_rate * block.astype(jnp.float32)
        ).astype(jnp.bfloat16)

    apply(me, sendbuf[me])
    for k, copy in enumerate(copies, 1):
        copy.wait()
        apply(lax.rem(me + n - k, n), recv[k])


def step(out_grad, proj_hi, proj_lo, first_moment, second_moment, projector, weight, n):
    pieces = 8
    hidden = out_grad.shape[1] // n
    rank = proj_hi.shape[1]
    rows = weight.shape[0]
    vmem = pl.BlockSpec(memory_space=pltpu.VMEM)
    return pl.pallas_call(
        functools.partial(step_kernel, n, pieces),
        out_shape=(
            jax.ShapeDtypeStruct(weight.shape, weight.dtype),
            jax.ShapeDtypeStruct((hidden, rank), jnp.float32),
            jax.ShapeDtypeStruct((hidden, rank), jnp.float32),
        ),
        in_specs=[vmem] * 7,
        out_specs=(vmem, vmem, vmem),
        scratch_shapes=[
            pltpu.VMEM((n, rank, hidden), jnp.bfloat16),
            pltpu.VMEM((n, rank, hidden), jnp.bfloat16),
            pltpu.VMEM((n, rank, hidden), jnp.bfloat16),
            pltpu.VMEM((rank, hidden), jnp.float32),
            pltpu.VMEM((rank, proj_hi.shape[0]), jnp.bfloat16),
            pltpu.VMEM((rank, proj_hi.shape[0]), jnp.bfloat16),
            pltpu.VMEM((hidden, rank), jnp.bfloat16),
            pltpu.VMEM((n, rows, hidden), jnp.bfloat16),
            pltpu.VMEM((n, rows, hidden), jnp.bfloat16),
            pltpu.VMEM((n, rows, hidden), jnp.bfloat16),
            pltpu.SemaphoreType.DMA(()),
            pltpu.SemaphoreType.DMA((pieces, n)),
            pltpu.SemaphoreType.DMA((pieces, n)),
            pltpu.SemaphoreType.DMA((n,)),
            pltpu.SemaphoreType.DMA((n,)),
        ],
        compiler_params=pltpu.CompilerParams(
            collective_id=2, has_side_effects=True, vmem_limit_bytes=64 * 1024 * 1024
        ),
    )(out_grad, proj_hi, proj_lo, first_moment, second_moment, projector, weight)


def chip_gather_kernel(
    acts_ref, proj_ref, hi_ref, lo_ref, q_buf, send_buf, recv, local_sem, send_sem, recv_sem
):
    me = lax.axis_index("tensor")
    core_peer = me + 1 - 2 * lax.rem(me, 2)
    chip_peer = lax.rem(me + 2, 4)
    barrier = pltpu.get_barrier_semaphore()
    for peer in (core_peer, chip_peer):
        pl.semaphore_signal(barrier, inc=1, device_id={"tensor": peer}, device_id_type=MESH_ID)
    q_buf[...] = jnp.dot(acts_ref[...], proj_ref[...], preferred_element_type=jnp.float32)
    local = pltpu.make_async_copy(q_buf, send_buf, local_sem)
    local.start()
    local.wait()
    pl.semaphore_wait(barrier, 2)

    def send(src, slot, peer):
        copy = pltpu.make_async_remote_copy(
            src_ref=src,
            dst_ref=recv.at[slot],
            send_sem=send_sem.at[slot],
            recv_sem=recv_sem.at[slot],
            device_id={"tensor": peer},
            device_id_type=MESH_ID,
        )
        copy.start()
        return copy

    def split(slot, piece):
        hi = piece.astype(jnp.bfloat16)
        hi_ref[slot] = hi
        lo_ref[slot] = (piece - hi.astype(jnp.float32)).astype(jnp.bfloat16)

    across = send(send_buf, 1, chip_peer)
    beside = send(send_buf, 0, core_peer)
    split(me, send_buf[...])
    across.wait()
    forward = send(recv.at[1], 2, core_peer)
    split(chip_peer, recv[1])
    beside.wait()
    split(core_peer, recv[0])
    forward.wait()
    split(3 - me, recv[2])


def chip_gather(acts, projector):
    shape = (acts.shape[0], projector.shape[1])
    vmem = pl.BlockSpec(memory_space=pltpu.VMEM)
    return pl.pallas_call(
        chip_gather_kernel,
        out_shape=(
            jax.ShapeDtypeStruct((4,) + shape, jnp.bfloat16),
            jax.ShapeDtypeStruct((4,) + shape, jnp.bfloat16),
        ),
        in_specs=[vmem, vmem],
        out_specs=(vmem, vmem),
        scratch_shapes=[
            pltpu.VMEM(shape, jnp.float32),
            pltpu.VMEM(shape, jnp.float32),
            pltpu.VMEM((3,) + shape, jnp.float32),
            pltpu.SemaphoreType.DMA(()),
            pltpu.SemaphoreType.DMA((3,)),
            pltpu.SemaphoreType.DMA((3,)),
        ],
        compiler_params=pltpu.CompilerParams(
            collective_id=1, has_side_effects=True, vmem_limit_bytes=48 * 1024 * 1024
        ),
    )(acts, projector)


def per_device(acts, out_grad, projector, weight, first_moment, second_moment):
    assert lax.axis_size("tensor") == 4
    proj_hi, proj_lo = chip_gather(acts, projector)
    proj_hi = proj_hi.reshape(-1, proj_hi.shape[2])
    proj_lo = proj_lo.reshape(-1, proj_lo.shape[2])
    new_weight, new_first, new_second = step(
        out_grad, proj_hi, proj_lo, first_moment[0], second_moment[0], projector, weight,
        lax.axis_size("dp"),
    )
    return (new_weight, new_first[None], new_second[None])


def solution(mesh):
    return jax.shard_map(
        per_device,
        mesh=mesh,
        in_specs=(
            P(("dp", "tensor"), None),
            P("dp", "tensor"),
            P(),
            P("dp", "tensor"),
            P("tensor", "dp", None),
            P("tensor", "dp", None),
        ),
        out_specs=(P("dp", "tensor"), P("tensor", "dp", None), P("tensor", "dp", None)),
        check_vma=False,
    )
```

```python
import functools

import jax
import jax.numpy as jnp
from jax import lax
from jax.experimental import pallas as pl
from jax.experimental.pallas import tpu as pltpu
from jax.sharding import PartitionSpec as P

beta_first = 0.9
beta_second = 0.95
adam_step = 10
epsilon = 1e-08
step_rate = 0.5

MESH_ID = pl.DeviceIdType.MESH


def adam_moments(lowgrad, first_moment, second_moment):
    new_first = beta_first * first_moment + (1.0 - beta_first) * lowgrad
    new_second = beta_second * second_moment + (1.0 - beta_second) * lowgrad * lowgrad
    corrected_first = new_first / (1.0 - beta_first**adam_step)
    corrected_second = new_second / (1.0 - beta_second**adam_step)
    direction = (corrected_first / (jnp.sqrt(corrected_second) + epsilon)).astype(jnp.bfloat16)
    return (new_first, new_second, direction)


def exchange_sum_kernel(n, pieces, part_ref, out_ref, recv, send_sem, recv_sem):
    me = lax.axis_index("dp")
    col = lax.axis_index("tensor")
    barrier = pltpu.get_barrier_semaphore()
    for k in range(1, n):
        pl.semaphore_signal(
            barrier, inc=1, device_id=(lax.rem(me + k, n), col), device_id_type=MESH_ID
        )
    pl.semaphore_wait(barrier, n - 1)
    piece = part_ref.shape[1] // pieces

    def part_copy(k, p):
        dest = lax.rem(me + k, n)
        span = pl.ds(pl.multiple_of(p * piece, piece), piece)
        return pltpu.make_async_remote_copy(
            src_ref=part_ref.at[dest, span],
            dst_ref=recv.at[k, span],
            send_sem=send_sem.at[p, k],
            recv_sem=recv_sem.at[p, k],
            device_id=(dest, col),
            device_id_type=MESH_ID,
        )

    def start_part(i, carry):
        part_copy(lax.rem(i, n - 1) + 1, i // (n - 1)).start()
        return carry

    lax.fori_loop(0, (n - 1) * pieces, start_part, 0)
    out_ref[...] = part_ref[me].astype(jnp.float32)

    def add_block(k, carry):
        for p in range(pieces):
            part_copy(k, p).wait()
        out_ref[...] += recv[k].astype(jnp.float32)
        return carry

    lax.fori_loop(1, n, add_block, 0)


def exchange_sum(part):
    n, rows, cols = part.shape
    pieces = 8
    return pl.pallas_call(
        functools.partial(exchange_sum_kernel, n, pieces),
        out_shape=jax.ShapeDtypeStruct((rows, cols), jnp.float32),
        in_specs=[pl.BlockSpec(memory_space=pltpu.VMEM)],
        out_specs=pl.BlockSpec(memory_space=pltpu.VMEM),
        scratch_shapes=[
            pltpu.VMEM((n, rows, cols), part.dtype),
            pltpu.SemaphoreType.DMA((pieces, n)),
            pltpu.SemaphoreType.DMA((pieces, n)),
        ],
        compiler_params=pltpu.CompilerParams(
            collective_id=0, has_side_effects=True, vmem_limit_bytes=48 * 1024 * 1024
        ),
    )(part)


def tail_kernel(
    n, blocks_ref, rest_ref, first_ref, second_ref, proj_ref, weight_ref,
    new_weight_ref, new_first_ref, new_second_ref,
    total, direction_ref, update, sendbuf, recv, local_sem, send_sem, recv_sem,
):
    me = lax.axis_index("dp")
    col = lax.axis_index("tensor")
    rows = sendbuf.shape[1]
    width = sendbuf.shape[2]
    barrier = pltpu.get_barrier_semaphore()
    for k in range(1, n):
        pl.semaphore_signal(
            barrier, inc=1, device_id=(lax.rem(me + k, n), col), device_id_type=MESH_ID
        )

    band = 16

    def rows_step(r, carry):
        rs = pl.ds(pl.multiple_of(r * band, band), band)
        lowgrad = blocks_ref[0, rs, :].astype(jnp.float32)
        for k in range(1, n):
            lowgrad += blocks_ref[k, rs, :].astype(jnp.float32)
        lowgrad = jnp.concatenate([lowgrad, rest_ref[rs, :]], axis=1)
        new_first, new_second, direction = adam_moments(
            lowgrad, first_ref[rs, :], second_ref[rs, :]
        )
        new_first_ref[rs, :] = new_first
        new_second_ref[rs, :] = new_second
        direction_ref[rs, :] = direction
        return carry

    lax.fori_loop(0, blocks_ref.shape[1] // band, rows_step, 0)

    update[...] = (
        lax.dot_general(
            proj_ref[...],
            direction_ref[...],
            (((1,), (1,)), ((), ())),
            preferred_element_type=jnp.float32,
        )
        .astype(jnp.bfloat16)
        .reshape(update.shape)
    )
    local = pltpu.make_async_copy(update, sendbuf, local_sem)
    local.start()
    local.wait()
    pl.semaphore_wait(barrier, n - 1)
    copies = []
    for k in range(1, n):
        dest = lax.rem(me + k, n)
        copy = pltpu.make_async_remote_copy(
            src_ref=sendbuf.at[dest],
            dst_ref=recv.at[k],
            send_sem=send_sem.at[k],
            recv_sem=recv_sem.at[k],
            device_id=(dest, col),
            device_id_type=MESH_ID,
        )
        copy.start()
        copies.append(copy)

    def apply(source, block):
        cols = pl.ds(pl.multiple_of(source * width, width), width)
        new_weight_ref[:, cols] = (
            weight_ref[:, cols].astype(jnp.float32) - step_rate * block.astype(jnp.float32)
        ).astype(jnp.bfloat16)

    apply(me, sendbuf[me])
    for k, copy in enumerate(copies, 1):
        copy.wait()
        apply(lax.rem(me + n - k, n), recv[k])


def tail(blocks, rest, first_moment, second_moment, projector, weight):
    n, hidden, rank = blocks.shape
    rank = rank + rest.shape[1]
    rows = weight.shape[0]
    vmem = pl.BlockSpec(memory_space=pltpu.VMEM)
    return pl.pallas_call(
        functools.partial(tail_kernel, n),
        out_shape=(
            jax.ShapeDtypeStruct(weight.shape, weight.dtype),
            jax.ShapeDtypeStruct((hidden, rank), jnp.float32),
            jax.ShapeDtypeStruct((hidden, rank), jnp.float32),
        ),
        in_specs=[vmem] * 6,
        out_specs=(vmem, vmem, vmem),
        scratch_shapes=[
            pltpu.VMEM((hidden, rank), jnp.float32),
            pltpu.VMEM((hidden, rank), jnp.bfloat16),
            pltpu.VMEM((n, rows, hidden), jnp.bfloat16),
            pltpu.VMEM((n, rows, hidden), jnp.bfloat16),
            pltpu.VMEM((n, rows, hidden), jnp.bfloat16),
            pltpu.SemaphoreType.DMA(()),
            pltpu.SemaphoreType.DMA((n,)),
            pltpu.SemaphoreType.DMA((n,)),
        ],
        compiler_params=pltpu.CompilerParams(
            collective_id=2, has_side_effects=True, vmem_limit_bytes=48 * 1024 * 1024
        ),
    )(blocks, rest, first_moment, second_moment, projector, weight)


def chip_gather_kernel(
    acts_ref, proj_ref, hi_ref, lo_ref, q_buf, send_buf, recv, local_sem, send_sem, recv_sem
):
    me = lax.axis_index("tensor")
    core_peer = me + 1 - 2 * lax.rem(me, 2)
    chip_peer = lax.rem(me + 2, 4)
    barrier = pltpu.get_barrier_semaphore()
    for peer in (core_peer, chip_peer):
        pl.semaphore_signal(barrier, inc=1, device_id={"tensor": peer}, device_id_type=MESH_ID)
    q_buf[...] = jnp.dot(acts_ref[...], proj_ref[...], preferred_element_type=jnp.float32)
    local = pltpu.make_async_copy(q_buf, send_buf, local_sem)
    local.start()
    local.wait()
    pl.semaphore_wait(barrier, 2)

    half = send_buf.shape[0] // 2

    def send(src, slot, peer, p):
        span = pl.ds(p * half, half)
        copy = pltpu.make_async_remote_copy(
            src_ref=src.at[span],
            dst_ref=recv.at[slot, span],
            send_sem=send_sem.at[slot, p],
            recv_sem=recv_sem.at[slot, p],
            device_id={"tensor": peer},
            device_id_type=MESH_ID,
        )
        copy.start()
        return copy

    def split(slot, piece):
        hi = piece.astype(jnp.bfloat16)
        hi_ref[slot] = hi
        lo_ref[slot] = (piece - hi.astype(jnp.float32)).astype(jnp.bfloat16)

    across = [send(send_buf, 1, chip_peer, p) for p in range(2)]
    beside = [send(send_buf, 0, core_peer, p) for p in range(2)]
    split(me, send_buf[...])
    forward = []
    for p in range(2):
        across[p].wait()
        forward.append(send(recv.at[1], 2, core_peer, p))
    split(chip_peer, recv[1])
    for copy in beside:
        copy.wait()
    split(core_peer, recv[0])
    for copy in forward:
        copy.wait()
    split(3 - me, recv[2])


def chip_gather(acts, projector):
    shape = (acts.shape[0], projector.shape[1])
    vmem = pl.BlockSpec(memory_space=pltpu.VMEM)
    return pl.pallas_call(
        chip_gather_kernel,
        out_shape=(
            jax.ShapeDtypeStruct((4,) + shape, jnp.bfloat16),
            jax.ShapeDtypeStruct((4,) + shape, jnp.bfloat16),
        ),
        in_specs=[vmem, vmem],
        out_specs=(vmem, vmem),
        scratch_shapes=[
            pltpu.VMEM(shape, jnp.float32),
            pltpu.VMEM(shape, jnp.float32),
            pltpu.VMEM((3,) + shape, jnp.float32),
            pltpu.SemaphoreType.DMA(()),
            pltpu.SemaphoreType.DMA((3, 2)),
            pltpu.SemaphoreType.DMA((3, 2)),
        ],
        compiler_params=pltpu.CompilerParams(
            collective_id=1, has_side_effects=True, vmem_limit_bytes=48 * 1024 * 1024
        ),
    )(acts, projector)


def per_device(acts, out_grad, projector, weight, first_moment, second_moment):
    assert lax.axis_size("tensor") == 4
    proj_hi, proj_lo = chip_gather(acts, projector)
    proj_hi = proj_hi.reshape(-1, proj_hi.shape[2])
    proj_lo = proj_lo.reshape(-1, proj_lo.shape[2])
    owners = lax.axis_size("dp")
    grad_blocks = out_grad.reshape(out_grad.shape[0], owners, -1)
    dims = (((0,), (0,)), ((), ()))
    half = proj_hi.shape[1] // 2

    def partial_of(cols):
        return (
            lax.dot_general(grad_blocks, proj_hi[:, cols], dims, preferred_element_type=jnp.float32)
            + lax.dot_general(grad_blocks, proj_lo[:, cols], dims, preferred_element_type=jnp.float32)
        ).astype(jnp.bfloat16)

    blocks = lax.all_to_all(
        partial_of(slice(0, half)), "dp", split_axis=0, concat_axis=0, tiled=True
    )
    rest = exchange_sum(partial_of(slice(half, None)))
    new_weight, new_first, new_second = tail(
        blocks, rest, first_moment[0], second_moment[0], projector, weight
    )
    return (new_weight, new_first[None], new_second[None])


def solution(mesh):
    return jax.shard_map(
        per_device,
        mesh=mesh,
        in_specs=(
            P(("dp", "tensor"), None),
            P("dp", "tensor"),
            P(),
            P("dp", "tensor"),
            P("tensor", "dp", None),
            P("tensor", "dp", None),
        ),
        out_specs=(P("dp", "tensor"), P("tensor", "dp", None), P("tensor", "dp", None)),
        check_vma=False,
    )
```

```python
import functools

import jax
import jax.numpy as jnp
from jax import lax
from jax.experimental import pallas as pl
from jax.experimental.pallas import tpu as pltpu
from jax.sharding import PartitionSpec as P

beta_first = 0.9
beta_second = 0.95
adam_step = 10
epsilon = 1e-08
step_rate = 0.5

MESH_ID = pl.DeviceIdType.MESH


def adam_moments(lowgrad, first_moment, second_moment):
    new_first = beta_first * first_moment + (1.0 - beta_first) * lowgrad
    new_second = beta_second * second_moment + (1.0 - beta_second) * lowgrad * lowgrad
    corrected_first = new_first / (1.0 - beta_first**adam_step)
    corrected_second = new_second / (1.0 - beta_second**adam_step)
    direction = (corrected_first / (jnp.sqrt(corrected_second) + epsilon)).astype(jnp.bfloat16)
    return (new_first, new_second, direction)


def tail_kernel(
    n, blocks_ref, first_ref, second_ref, proj_ref, weight_ref,
    new_weight_ref, new_first_ref, new_second_ref,
    total, direction_ref, update, sendbuf, recv, local_sem, send_sem, recv_sem,
):
    me = lax.axis_index("dp")
    col = lax.axis_index("tensor")
    rows = sendbuf.shape[1]
    width = sendbuf.shape[2]
    barrier = pltpu.get_barrier_semaphore()
    for k in range(1, n):
        pl.semaphore_signal(
            barrier, inc=1, device_id=(lax.rem(me + k, n), col), device_id_type=MESH_ID
        )

    band = 16

    def rows_step(r, carry):
        rs = pl.ds(pl.multiple_of(r * band, band), band)
        lowgrad = blocks_ref[0, rs, :].astype(jnp.float32)
        for k in range(1, n):
            lowgrad += blocks_ref[k, rs, :].astype(jnp.float32)
        new_first, new_second, direction = adam_moments(
            lowgrad, first_ref[rs, :], second_ref[rs, :]
        )
        new_first_ref[rs, :] = new_first
        new_second_ref[rs, :] = new_second
        direction_ref[rs, :] = direction
        return carry

    lax.fori_loop(0, blocks_ref.shape[1] // band, rows_step, 0)

    update[...] = (
        lax.dot_general(
            proj_ref[...],
            direction_ref[...],
            (((1,), (1,)), ((), ())),
            preferred_element_type=jnp.float32,
        )
        .astype(jnp.bfloat16)
        .reshape(update.shape)
    )
    local = pltpu.make_async_copy(update, sendbuf, local_sem)
    local.start()
    local.wait()
    pl.semaphore_wait(barrier, n - 1)
    copies = []
    for k in range(1, n):
        dest = lax.rem(me + k, n)
        copy = pltpu.make_async_remote_copy(
            src_ref=sendbuf.at[dest],
            dst_ref=recv.at[k],
            send_sem=send_sem.at[k],
            recv_sem=recv_sem.at[k],
            device_id=(dest, col),
            device_id_type=MESH_ID,
        )
        copy.start()
        copies.append(copy)

    def apply(source, block):
        cols = pl.ds(pl.multiple_of(source * width, width), width)
        new_weight_ref[:, cols] = (
            weight_ref[:, cols].astype(jnp.float32) - step_rate * block.astype(jnp.float32)
        ).astype(jnp.bfloat16)

    apply(me, sendbuf[me])
    for k, copy in enumerate(copies, 1):
        copy.wait()
        apply(lax.rem(me + n - k, n), recv[k])


def tail(blocks, first_moment, second_moment, projector, weight):
    n, hidden, rank = blocks.shape
    rows = weight.shape[0]
    vmem = pl.BlockSpec(memory_space=pltpu.VMEM)
    return pl.pallas_call(
        functools.partial(tail_kernel, n),
        out_shape=(
            jax.ShapeDtypeStruct(weight.shape, weight.dtype),
            jax.ShapeDtypeStruct((hidden, rank), jnp.float32),
            jax.ShapeDtypeStruct((hidden, rank), jnp.float32),
        ),
        in_specs=[vmem] * 5,
        out_specs=(vmem, vmem, vmem),
        scratch_shapes=[
            pltpu.VMEM((hidden, rank), jnp.float32),
            pltpu.VMEM((hidden, rank), jnp.bfloat16),
            pltpu.VMEM((n, rows, hidden), jnp.bfloat16),
            pltpu.VMEM((n, rows, hidden), jnp.bfloat16),
            pltpu.VMEM((n, rows, hidden), jnp.bfloat16),
            pltpu.SemaphoreType.DMA(()),
            pltpu.SemaphoreType.DMA((n,)),
            pltpu.SemaphoreType.DMA((n,)),
        ],
        compiler_params=pltpu.CompilerParams(
            collective_id=2, has_side_effects=True, vmem_limit_bytes=48 * 1024 * 1024
        ),
    )(blocks, first_moment, second_moment, projector, weight)


def chip_gather_kernel(
    acts_ref, proj_ref, hi_ref, q_buf, send_buf, recv, local_sem, send_sem, recv_sem
):
    me = lax.axis_index("tensor")
    core_peer = me + 1 - 2 * lax.rem(me, 2)
    chip_peer = lax.rem(me + 2, 4)
    barrier = pltpu.get_barrier_semaphore()
    for peer in (core_peer, chip_peer):
        pl.semaphore_signal(barrier, inc=1, device_id={"tensor": peer}, device_id_type=MESH_ID)
    q_buf[...] = jnp.dot(acts_ref[...], proj_ref[...], preferred_element_type=jnp.float32)
    local = pltpu.make_async_copy(q_buf, send_buf, local_sem)
    local.start()
    local.wait()
    pl.semaphore_wait(barrier, 2)

    half = send_buf.shape[0] // 2

    def send(src, slot, peer, p):
        span = pl.ds(p * half, half)
        copy = pltpu.make_async_remote_copy(
            src_ref=src.at[span],
            dst_ref=recv.at[slot, span],
            send_sem=send_sem.at[slot, p],
            recv_sem=recv_sem.at[slot, p],
            device_id={"tensor": peer},
            device_id_type=MESH_ID,
        )
        copy.start()
        return copy

    def split(slot, piece):
        hi_ref[slot] = piece.astype(jnp.bfloat16)

    across = [send(send_buf, 1, chip_peer, p) for p in range(2)]
    beside = [send(send_buf, 0, core_peer, p) for p in range(2)]
    split(me, send_buf[...])
    forward = []
    for p in range(2):
        across[p].wait()
        forward.append(send(recv.at[1], 2, core_peer, p))
    split(chip_peer, recv[1])
    for copy in beside:
        copy.wait()
    split(core_peer, recv[0])
    for copy in forward:
        copy.wait()
    split(3 - me, recv[2])


def chip_gather(acts, projector):
    shape = (acts.shape[0], projector.shape[1])
    vmem = pl.BlockSpec(memory_space=pltpu.VMEM)
    return pl.pallas_call(
        chip_gather_kernel,
        out_shape=jax.ShapeDtypeStruct((4,) + shape, jnp.bfloat16),
        in_specs=[vmem, vmem],
        out_specs=vmem,
        scratch_shapes=[
            pltpu.VMEM(shape, jnp.float32),
            pltpu.VMEM(shape, jnp.float32),
            pltpu.VMEM((3,) + shape, jnp.float32),
            pltpu.SemaphoreType.DMA(()),
            pltpu.SemaphoreType.DMA((3, 2)),
            pltpu.SemaphoreType.DMA((3, 2)),
        ],
        compiler_params=pltpu.CompilerParams(
            collective_id=1, has_side_effects=True, vmem_limit_bytes=48 * 1024 * 1024
        ),
    )(acts, projector)


def per_device(acts, out_grad, projector, weight, first_moment, second_moment):
    assert lax.axis_size("tensor") == 4
    proj_hi = chip_gather(acts, projector)
    proj_hi = proj_hi.reshape(-1, proj_hi.shape[2])
    owners = lax.axis_size("dp")
    grad_blocks = out_grad.reshape(out_grad.shape[0], owners, -1)
    dims = (((0,), (0,)), ((), ()))
    partial = lax.dot_general(grad_blocks, proj_hi, dims, preferred_element_type=jnp.float32)
    blocks = lax.all_to_all(
        partial.astype(jnp.bfloat16), "dp", split_axis=0, concat_axis=0, tiled=True
    )
    new_weight, new_first, new_second = tail(
        blocks, first_moment[0], second_moment[0], projector, weight
    )
    return (new_weight, new_first[None], new_second[None])


def solution(mesh):
    return jax.shard_map(
        per_device,
        mesh=mesh,
        in_specs=(
            P(("dp", "tensor"), None),
            P("dp", "tensor"),
            P(),
            P("dp", "tensor"),
            P("tensor", "dp", None),
            P("tensor", "dp", None),
        ),
        out_specs=(P("dp", "tensor"), P("tensor", "dp", None), P("tensor", "dp", None)),
        check_vma=False,
    )
```

```python
import functools

import jax
import jax.numpy as jnp
from jax import lax
from jax.experimental import pallas as pl
from jax.experimental.pallas import tpu as pltpu
from jax.sharding import PartitionSpec as P

beta_first = 0.9
beta_second = 0.95
adam_step = 10
epsilon = 1e-08
step_rate = 0.5

MESH_ID = pl.DeviceIdType.MESH


def adam_moments(lowgrad, first_moment, second_moment):
    new_first = beta_first * first_moment + (1.0 - beta_first) * lowgrad
    new_second = beta_second * second_moment + (1.0 - beta_second) * lowgrad * lowgrad
    corrected_first = new_first / (1.0 - beta_first**adam_step)
    corrected_second = new_second / (1.0 - beta_second**adam_step)
    direction = (corrected_first / (jnp.sqrt(corrected_second) + epsilon)).astype(jnp.bfloat16)
    return (new_first, new_second, direction)


def tail_kernel(
    n, blocks_ref, first_ref, second_ref, proj_ref, weight_ref,
    new_weight_ref, new_first_ref, new_second_ref,
    total, direction_ref, update, sendbuf, recv, local_sem, send_sem, recv_sem,
):
    me = lax.axis_index("dp")
    col = lax.axis_index("tensor")
    rows = sendbuf.shape[1]
    width = sendbuf.shape[2]
    barrier = pltpu.get_barrier_semaphore()
    for k in range(1, n):
        pl.semaphore_signal(
            barrier, inc=1, device_id=(lax.rem(me + k, n), col), device_id_type=MESH_ID
        )

    band = 16

    def rows_step(r, carry):
        rs = pl.ds(pl.multiple_of(r * band, band), band)
        lowgrad = blocks_ref[0, rs, :].astype(jnp.float32)
        for k in range(1, n):
            lowgrad += blocks_ref[k, rs, :].astype(jnp.float32)
        new_first, new_second, direction = adam_moments(
            lowgrad, first_ref[rs, :], second_ref[rs, :]
        )
        new_first_ref[rs, :] = new_first
        new_second_ref[rs, :] = new_second
        direction_ref[rs, :] = direction
        return carry

    lax.fori_loop(0, blocks_ref.shape[1] // band, rows_step, 0)

    update[...] = (
        lax.dot_general(
            proj_ref[...],
            direction_ref[...],
            (((1,), (1,)), ((), ())),
            preferred_element_type=jnp.float32,
        )
        .astype(jnp.bfloat16)
        .reshape(update.shape)
    )
    local = pltpu.make_async_copy(update, sendbuf, local_sem)
    local.start()
    local.wait()
    pl.semaphore_wait(barrier, n - 1)
    copies = []
    for k in range(1, n):
        dest = lax.rem(me + k, n)
        copy = pltpu.make_async_remote_copy(
            src_ref=sendbuf.at[dest],
            dst_ref=recv.at[k],
            send_sem=send_sem.at[k],
            recv_sem=recv_sem.at[k],
            device_id=(dest, col),
            device_id_type=MESH_ID,
        )
        copy.start()
        copies.append(copy)

    def apply(source, block):
        cols = pl.ds(pl.multiple_of(source * width, width), width)
        new_weight_ref[:, cols] = (
            weight_ref[:, cols].astype(jnp.float32) - step_rate * block.astype(jnp.float32)
        ).astype(jnp.bfloat16)

    apply(me, sendbuf[me])
    for k, copy in enumerate(copies, 1):
        copy.wait()
        apply(lax.rem(me + n - k, n), recv[k])


def tail(blocks, first_moment, second_moment, projector, weight):
    n, hidden, rank = blocks.shape
    rows = weight.shape[0]
    vmem = pl.BlockSpec(memory_space=pltpu.VMEM)
    return pl.pallas_call(
        functools.partial(tail_kernel, n),
        out_shape=(
            jax.ShapeDtypeStruct(weight.shape, weight.dtype),
            jax.ShapeDtypeStruct((hidden, rank), jnp.float32),
            jax.ShapeDtypeStruct((hidden, rank), jnp.float32),
        ),
        in_specs=[vmem] * 5,
        out_specs=(vmem, vmem, vmem),
        scratch_shapes=[
            pltpu.VMEM((hidden, rank), jnp.float32),
            pltpu.VMEM((hidden, rank), jnp.bfloat16),
            pltpu.VMEM((n, rows, hidden), jnp.bfloat16),
            pltpu.VMEM((n, rows, hidden), jnp.bfloat16),
            pltpu.VMEM((n, rows, hidden), jnp.bfloat16),
            pltpu.SemaphoreType.DMA(()),
            pltpu.SemaphoreType.DMA((n,)),
            pltpu.SemaphoreType.DMA((n,)),
        ],
        compiler_params=pltpu.CompilerParams(
            collective_id=2, has_side_effects=True, vmem_limit_bytes=48 * 1024 * 1024
        ),
    )(blocks, first_moment, second_moment, projector, weight)


def chip_gather_kernel(
    acts_ref, proj_ref, hi_ref, q_buf, send_buf, recv, local_sem, send_sem, recv_sem
):
    me = lax.axis_index("tensor")
    core_peer = me + 1 - 2 * lax.rem(me, 2)
    chip_peer = lax.rem(me + 2, 4)
    barrier = pltpu.get_barrier_semaphore()
    for peer in (core_peer, chip_peer):
        pl.semaphore_signal(barrier, inc=1, device_id={"tensor": peer}, device_id_type=MESH_ID)
    q_buf[...] = jnp.dot(acts_ref[...], proj_ref[...], preferred_element_type=jnp.float32).astype(
        jnp.bfloat16
    )
    local = pltpu.make_async_copy(q_buf, send_buf, local_sem)
    local.start()
    local.wait()
    pl.semaphore_wait(barrier, 2)

    half = send_buf.shape[0] // 2

    def send(src, slot, peer, p):
        span = pl.ds(p * half, half)
        copy = pltpu.make_async_remote_copy(
            src_ref=src.at[span],
            dst_ref=recv.at[slot, span],
            send_sem=send_sem.at[slot, p],
            recv_sem=recv_sem.at[slot, p],
            device_id={"tensor": peer},
            device_id_type=MESH_ID,
        )
        copy.start()
        return copy

    def split(slot, piece):
        hi_ref[slot] = piece

    across = [send(send_buf, 1, chip_peer, p) for p in range(2)]
    beside = [send(send_buf, 0, core_peer, p) for p in range(2)]
    split(me, send_buf[...])
    forward = []
    for p in range(2):
        across[p].wait()
        forward.append(send(recv.at[1], 2, core_peer, p))
    split(chip_peer, recv[1])
    for copy in beside:
        copy.wait()
    split(core_peer, recv[0])
    for copy in forward:
        copy.wait()
    split(3 - me, recv[2])


def chip_gather(acts, projector):
    shape = (acts.shape[0], projector.shape[1])
    vmem = pl.BlockSpec(memory_space=pltpu.VMEM)
    return pl.pallas_call(
        chip_gather_kernel,
        out_shape=jax.ShapeDtypeStruct((4,) + shape, jnp.bfloat16),
        in_specs=[vmem, vmem],
        out_specs=vmem,
        scratch_shapes=[
            pltpu.VMEM(shape, jnp.bfloat16),
            pltpu.VMEM(shape, jnp.bfloat16),
            pltpu.VMEM((3,) + shape, jnp.bfloat16),
            pltpu.SemaphoreType.DMA(()),
            pltpu.SemaphoreType.DMA((3, 2)),
            pltpu.SemaphoreType.DMA((3, 2)),
        ],
        compiler_params=pltpu.CompilerParams(
            collective_id=1, has_side_effects=True, vmem_limit_bytes=48 * 1024 * 1024
        ),
    )(acts, projector)


def per_device(acts, out_grad, projector, weight, first_moment, second_moment):
    assert lax.axis_size("tensor") == 4
    proj_hi = chip_gather(acts, projector)
    proj_hi = proj_hi.reshape(-1, proj_hi.shape[2])
    owners = lax.axis_size("dp")
    grad_blocks = out_grad.reshape(out_grad.shape[0], owners, -1)
    dims = (((0,), (0,)), ((), ()))
    partial = lax.dot_general(grad_blocks, proj_hi, dims, preferred_element_type=jnp.float32)
    blocks = lax.all_to_all(
        partial.astype(jnp.bfloat16), "dp", split_axis=0, concat_axis=0, tiled=True
    )
    new_weight, new_first, new_second = tail(
        blocks, first_moment[0], second_moment[0], projector, weight
    )
    return (new_weight, new_first[None], new_second[None])


def solution(mesh):
    return jax.shard_map(
        per_device,
        mesh=mesh,
        in_specs=(
            P(("dp", "tensor"), None),
            P("dp", "tensor"),
            P(),
            P("dp", "tensor"),
            P("tensor", "dp", None),
            P("tensor", "dp", None),
        ),
        out_specs=(P("dp", "tensor"), P("tensor", "dp", None), P("tensor", "dp", None)),
        check_vma=False,
    )
```

```python
import functools

import jax
import jax.numpy as jnp
from jax import lax
from jax.experimental import pallas as pl
from jax.experimental.pallas import tpu as pltpu
from jax.sharding import PartitionSpec as P

beta_first = 0.9
beta_second = 0.95
adam_step = 10
epsilon = 1e-08
step_rate = 0.5

MESH_ID = pl.DeviceIdType.MESH


def adam_moments(lowgrad, first_moment, second_moment):
    new_first = beta_first * first_moment + (1.0 - beta_first) * lowgrad
    new_second = beta_second * second_moment + (1.0 - beta_second) * lowgrad * lowgrad
    corrected_first = new_first / (1.0 - beta_first**adam_step)
    corrected_second = new_second / (1.0 - beta_second**adam_step)
    direction = (corrected_first / (jnp.sqrt(corrected_second) + epsilon)).astype(jnp.bfloat16)
    return (new_first, new_second, direction)


def tail_kernel(
    n, blocks_ref, first_ref, second_ref, proj_ref, weight_ref,
    new_weight_ref, new_first_ref, new_second_ref,
    total, direction_ref, update, sendbuf, recv, local_sem, send_sem, recv_sem,
):
    me = lax.axis_index("dp")
    col = lax.axis_index("tensor")
    rows = sendbuf.shape[1]
    width = sendbuf.shape[2]
    barrier = pltpu.get_barrier_semaphore()
    for k in range(1, n):
        pl.semaphore_signal(
            barrier, inc=1, device_id=(lax.rem(me + k, n), col), device_id_type=MESH_ID
        )

    band = 16

    def rows_step(r, carry):
        rs = pl.ds(pl.multiple_of(r * band, band), band)
        lowgrad = blocks_ref[0, rs, :].astype(jnp.float32)
        for k in range(1, n):
            lowgrad += blocks_ref[k, rs, :].astype(jnp.float32)
        new_first, new_second, direction = adam_moments(
            lowgrad, first_ref[rs, :], second_ref[rs, :]
        )
        new_first_ref[rs, :] = new_first
        new_second_ref[rs, :] = new_second
        direction_ref[rs, :] = direction
        return carry

    lax.fori_loop(0, blocks_ref.shape[1] // band, rows_step, 0)

    update[...] = (
        lax.dot_general(
            proj_ref[...],
            direction_ref[...],
            (((1,), (1,)), ((), ())),
            preferred_element_type=jnp.float32,
        )
        .astype(jnp.bfloat16)
        .reshape(update.shape)
    )
    local = pltpu.make_async_copy(update, sendbuf, local_sem)
    local.start()
    local.wait()
    pl.semaphore_wait(barrier, n - 1)
    copies = []
    for k in range(1, n):
        dest = lax.rem(me + k, n)
        copy = pltpu.make_async_remote_copy(
            src_ref=sendbuf.at[dest],
            dst_ref=recv.at[k],
            send_sem=send_sem.at[k],
            recv_sem=recv_sem.at[k],
            device_id=(dest, col),
            device_id_type=MESH_ID,
        )
        copy.start()
        copies.append(copy)

    def apply(source, block):
        cols = pl.ds(pl.multiple_of(source * width, width), width)
        new_weight_ref[:, cols] = (
            weight_ref[:, cols].astype(jnp.float32) - step_rate * block.astype(jnp.float32)
        ).astype(jnp.bfloat16)

    apply(me, sendbuf[me])
    for k, copy in enumerate(copies, 1):
        copy.wait()
        apply(lax.rem(me + n - k, n), recv[k])


def tail(blocks, first_moment, second_moment, projector, weight):
    n, hidden, rank = blocks.shape
    rows = weight.shape[0]
    vmem = pl.BlockSpec(memory_space=pltpu.VMEM)
    return pl.pallas_call(
        functools.partial(tail_kernel, n),
        out_shape=(
            jax.ShapeDtypeStruct(weight.shape, weight.dtype),
            jax.ShapeDtypeStruct((hidden, rank), jnp.float32),
            jax.ShapeDtypeStruct((hidden, rank), jnp.float32),
        ),
        in_specs=[vmem] * 5,
        out_specs=(vmem, vmem, vmem),
        scratch_shapes=[
            pltpu.VMEM((hidden, rank), jnp.float32),
            pltpu.VMEM((hidden, rank), jnp.bfloat16),
            pltpu.VMEM((n, rows, hidden), jnp.bfloat16),
            pltpu.VMEM((n, rows, hidden), jnp.bfloat16),
            pltpu.VMEM((n, rows, hidden), jnp.bfloat16),
            pltpu.SemaphoreType.DMA(()),
            pltpu.SemaphoreType.DMA((n,)),
            pltpu.SemaphoreType.DMA((n,)),
        ],
        compiler_params=pltpu.CompilerParams(
            collective_id=2, has_side_effects=True, vmem_limit_bytes=48 * 1024 * 1024
        ),
    )(blocks, first_moment, second_moment, projector, weight)


def chip_gather_kernel(
    acts_ref, proj_ref, hi_ref, acts_v, proj_v, q_acc, q_buf, send_buf, recv,
    load_sem, local_sem, send_sem, recv_sem,
):
    me = lax.axis_index("tensor")
    core_peer = me + 1 - 2 * lax.rem(me, 2)
    chip_peer = lax.rem(me + 2, 4)
    barrier = pltpu.get_barrier_semaphore()
    for peer in (core_peer, chip_peer):
        pl.semaphore_signal(barrier, inc=1, device_id={"tensor": peer}, device_id_type=MESH_ID)
    chunks = proj_v.shape[0]
    depth = proj_v.shape[1]
    loads = [pltpu.make_async_copy(acts_ref, acts_v, load_sem.at[chunks])]
    for i in range(chunks):
        loads.append(
            pltpu.make_async_copy(proj_ref.at[pl.ds(i * depth, depth)], proj_v.at[i], load_sem.at[i])
        )
    for load in loads:
        load.start()
    loads[0].wait()
    for i in range(chunks):
        loads[i + 1].wait()
        term = jnp.dot(
            acts_v[:, pl.ds(i * depth, depth)], proj_v[i], preferred_element_type=jnp.float32
        )
        if i == 0:
            q_acc[...] = term
        else:
            q_acc[...] += term
    q_buf[...] = q_acc[...].astype(jnp.bfloat16)
    local = pltpu.make_async_copy(q_buf, send_buf, local_sem)
    local.start()
    local.wait()
    pl.semaphore_wait(barrier, 2)

    half = send_buf.shape[0] // 2

    def send(src, slot, peer, p):
        span = pl.ds(p * half, half)
        copy = pltpu.make_async_remote_copy(
            src_ref=src.at[span],
            dst_ref=recv.at[slot, span],
            send_sem=send_sem.at[slot, p],
            recv_sem=recv_sem.at[slot, p],
            device_id={"tensor": peer},
            device_id_type=MESH_ID,
        )
        copy.start()
        return copy

    def split(slot, piece):
        hi_ref[slot] = piece

    across = [send(send_buf, 1, chip_peer, p) for p in range(2)]
    beside = [send(send_buf, 0, core_peer, p) for p in range(2)]
    split(me, send_buf[...])
    forward = []
    for p in range(2):
        across[p].wait()
        forward.append(send(recv.at[1], 2, core_peer, p))
    split(chip_peer, recv[1])
    for copy in beside:
        copy.wait()
    split(core_peer, recv[0])
    for copy in forward:
        copy.wait()
    split(3 - me, recv[2])


def chip_gather(acts, projector):
    shape = (acts.shape[0], projector.shape[1])
    chunks = 4
    depth = projector.shape[0] // chunks
    vmem = pl.BlockSpec(memory_space=pltpu.VMEM)
    hbm = pl.BlockSpec(memory_space=pl.ANY)
    return pl.pallas_call(
        chip_gather_kernel,
        out_shape=jax.ShapeDtypeStruct((4,) + shape, jnp.bfloat16),
        in_specs=[hbm, hbm],
        out_specs=vmem,
        scratch_shapes=[
            pltpu.VMEM(acts.shape, acts.dtype),
            pltpu.VMEM((chunks, depth, shape[1]), projector.dtype),
            pltpu.VMEM(shape, jnp.float32),
            pltpu.VMEM(shape, jnp.bfloat16),
            pltpu.VMEM(shape, jnp.bfloat16),
            pltpu.VMEM((3,) + shape, jnp.bfloat16),
            pltpu.SemaphoreType.DMA((chunks + 1,)),
            pltpu.SemaphoreType.DMA(()),
            pltpu.SemaphoreType.DMA((3, 2)),
            pltpu.SemaphoreType.DMA((3, 2)),
        ],
        compiler_params=pltpu.CompilerParams(
            collective_id=1, has_side_effects=True, vmem_limit_bytes=48 * 1024 * 1024
        ),
    )(acts, projector)


def per_device(acts, out_grad, projector, weight, first_moment, second_moment):
    assert lax.axis_size("tensor") == 4
    proj_hi = chip_gather(acts, projector)
    proj_hi = proj_hi.reshape(-1, proj_hi.shape[2])
    owners = lax.axis_size("dp")
    grad_blocks = out_grad.reshape(out_grad.shape[0], owners, -1)
    dims = (((0,), (0,)), ((), ()))
    partial = lax.dot_general(grad_blocks, proj_hi, dims, preferred_element_type=jnp.float32)
    blocks = lax.all_to_all(
        partial.astype(jnp.bfloat16), "dp", split_axis=0, concat_axis=0, tiled=True
    )
    new_weight, new_first, new_second = tail(
        blocks, first_moment[0], second_moment[0], projector, weight
    )
    return (new_weight, new_first[None], new_second[None])


def solution(mesh):
    return jax.shard_map(
        per_device,
        mesh=mesh,
        in_specs=(
            P(("dp", "tensor"), None),
            P("dp", "tensor"),
            P(),
            P("dp", "tensor"),
            P("tensor", "dp", None),
            P("tensor", "dp", None),
        ),
        out_specs=(P("dp", "tensor"), P("tensor", "dp", None), P("tensor", "dp", None)),
        check_vma=False,
    )
```

```python
import functools

import jax
import jax.numpy as jnp
from jax import lax
from jax.experimental import pallas as pl
from jax.experimental.pallas import tpu as pltpu
from jax.sharding import PartitionSpec as P

beta_first = 0.9
beta_second = 0.95
adam_step = 10
epsilon = 1e-08
step_rate = 0.5

MESH_ID = pl.DeviceIdType.MESH


def adam_moments(lowgrad, first_moment, second_moment):
    new_first = beta_first * first_moment + (1.0 - beta_first) * lowgrad
    new_second = beta_second * second_moment + (1.0 - beta_second) * lowgrad * lowgrad
    corrected_first = new_first / (1.0 - beta_first**adam_step)
    corrected_second = new_second / (1.0 - beta_second**adam_step)
    direction = (corrected_first / (jnp.sqrt(corrected_second) + epsilon)).astype(jnp.bfloat16)
    return (new_first, new_second, direction)


def tail_kernel(
    n, blocks_ref, first_ref, second_ref, proj_ref, weight_ref,
    new_weight_ref, new_first_ref, new_second_ref,
    total, direction_ref, update, sendbuf, recv, local_sem, send_sem, recv_sem,
):
    me = lax.axis_index("dp")
    col = lax.axis_index("tensor")
    rows = sendbuf.shape[1]
    width = sendbuf.shape[2]
    barrier = pltpu.get_barrier_semaphore()
    for k in range(1, n):
        pl.semaphore_signal(
            barrier, inc=1, device_id=(lax.rem(me + k, n), col), device_id_type=MESH_ID
        )

    band = 16

    def rows_step(r, carry):
        rs = pl.ds(pl.multiple_of(r * band, band), band)
        lowgrad = blocks_ref[0, rs, :].astype(jnp.float32)
        for k in range(1, n):
            lowgrad += blocks_ref[k, rs, :].astype(jnp.float32)
        new_first, new_second, direction = adam_moments(
            lowgrad, first_ref[rs, :], second_ref[rs, :]
        )
        new_first_ref[rs, :] = new_first
        new_second_ref[rs, :] = new_second
        direction_ref[rs, :] = direction
        return carry

    lax.fori_loop(0, blocks_ref.shape[1] // band, rows_step, 0)

    update[...] = (
        lax.dot_general(
            proj_ref[...],
            direction_ref[...],
            (((1,), (1,)), ((), ())),
            preferred_element_type=jnp.float32,
        )
        .astype(jnp.bfloat16)
        .reshape(update.shape)
    )
    local = pltpu.make_async_copy(update, sendbuf, local_sem)
    local.start()
    local.wait()
    pl.semaphore_wait(barrier, n - 1)
    copies = []
    for k in range(1, n):
        dest = lax.rem(me + k, n)
        copy = pltpu.make_async_remote_copy(
            src_ref=sendbuf.at[dest],
            dst_ref=recv.at[k],
            send_sem=send_sem.at[k],
            recv_sem=recv_sem.at[k],
            device_id=(dest, col),
            device_id_type=MESH_ID,
        )
        copy.start()
        copies.append(copy)

    def apply(source, block):
        cols = pl.ds(pl.multiple_of(source * width, width), width)
        new_weight_ref[:, cols] = (
            weight_ref[:, cols].astype(jnp.float32) - step_rate * block.astype(jnp.float32)
        ).astype(jnp.bfloat16)

    apply(me, sendbuf[me])
    for k, copy in enumerate(copies, 1):
        copy.wait()
        apply(lax.rem(me + n - k, n), recv[k])


def tail(blocks, first_moment, second_moment, projector, weight):
    n, hidden, rank = blocks.shape
    rows = weight.shape[0]
    vmem = pl.BlockSpec(memory_space=pltpu.VMEM)
    return pl.pallas_call(
        functools.partial(tail_kernel, n),
        out_shape=(
            jax.ShapeDtypeStruct(weight.shape, weight.dtype),
            jax.ShapeDtypeStruct((hidden, rank), jnp.float32),
            jax.ShapeDtypeStruct((hidden, rank), jnp.float32),
        ),
        in_specs=[vmem] * 5,
        out_specs=(vmem, vmem, vmem),
        scratch_shapes=[
            pltpu.VMEM((hidden, rank), jnp.float32),
            pltpu.VMEM((hidden, rank), jnp.bfloat16),
            pltpu.VMEM((n, rows, hidden), jnp.bfloat16),
            pltpu.VMEM((n, rows, hidden), jnp.bfloat16),
            pltpu.VMEM((n, rows, hidden), jnp.bfloat16),
            pltpu.SemaphoreType.DMA(()),
            pltpu.SemaphoreType.DMA((n,)),
            pltpu.SemaphoreType.DMA((n,)),
        ],
        compiler_params=pltpu.CompilerParams(
            collective_id=2, has_side_effects=True, vmem_limit_bytes=48 * 1024 * 1024
        ),
    )(blocks, first_moment, second_moment, projector, weight)


def chip_gather_kernel(
    acts_ref, proj_ref, hi_ref, acts_v, proj_v, q_acc, q_buf, send_buf, recv,
    load_sem, local_sem, send_sem, recv_sem,
):
    me = lax.axis_index("tensor")
    core_peer = me + 1 - 2 * lax.rem(me, 2)
    chip_peer = lax.rem(me + 2, 4)
    barrier = pltpu.get_barrier_semaphore()
    for peer in (core_peer, chip_peer):
        pl.semaphore_signal(barrier, inc=1, device_id={"tensor": peer}, device_id_type=MESH_ID)
    chunks = proj_v.shape[0]
    depth = proj_v.shape[1]
    loads = [pltpu.make_async_copy(acts_ref, acts_v, load_sem.at[chunks])]
    for i in range(chunks):
        loads.append(
            pltpu.make_async_copy(proj_ref.at[pl.ds(i * depth, depth)], proj_v.at[i], load_sem.at[i])
        )
    for load in loads:
        load.start()
    loads[0].wait()
    for i in range(chunks):
        loads[i + 1].wait()
        term = jnp.dot(
            acts_v[:, pl.ds(i * depth, depth)], proj_v[i], preferred_element_type=jnp.float32
        )
        if i == 0:
            q_acc[...] = term
        else:
            q_acc[...] += term
    q_buf[...] = q_acc[...].astype(jnp.bfloat16)
    local = pltpu.make_async_copy(q_buf, send_buf, local_sem)
    local.start()
    local.wait()
    pl.semaphore_wait(barrier, 2)

    half = send_buf.shape[0] // 2

    def send(src, slot, peer, p):
        span = pl.ds(p * half, half)
        copy = pltpu.make_async_remote_copy(
            src_ref=src.at[span],
            dst_ref=recv.at[slot, span],
            send_sem=send_sem.at[slot, p],
            recv_sem=recv_sem.at[slot, p],
            device_id={"tensor": peer},
            device_id_type=MESH_ID,
        )
        copy.start()
        return copy

    def split(slot, piece):
        hi_ref[slot] = piece

    across = [send(send_buf, 1, chip_peer, p) for p in range(2)]
    beside = [send(send_buf, 0, core_peer, p) for p in range(2)]
    split(me, send_buf[...])
    forward = []
    for p in range(2):
        across[p].wait()
        forward.append(send(recv.at[1], 2, core_peer, p))
    split(chip_peer, recv[1])
    for copy in beside:
        copy.wait()
    split(core_peer, recv[0])
    for copy in forward:
        copy.wait()
    split(3 - me, recv[2])


def chip_gather(acts, projector):
    shape = (acts.shape[0], projector.shape[1])
    chunks = 4
    depth = projector.shape[0] // chunks
    vmem = pl.BlockSpec(memory_space=pltpu.VMEM)
    hbm = pl.BlockSpec(memory_space=pl.ANY)
    return pl.pallas_call(
        chip_gather_kernel,
        out_shape=jax.ShapeDtypeStruct((4,) + shape, jnp.bfloat16),
        in_specs=[hbm, hbm],
        out_specs=vmem,
        scratch_shapes=[
            pltpu.VMEM(acts.shape, acts.dtype),
            pltpu.VMEM((chunks, depth, shape[1]), projector.dtype),
            pltpu.VMEM(shape, jnp.float32),
            pltpu.VMEM(shape, jnp.bfloat16),
            pltpu.VMEM(shape, jnp.bfloat16),
            pltpu.VMEM((3,) + shape, jnp.bfloat16),
            pltpu.SemaphoreType.DMA((chunks + 1,)),
            pltpu.SemaphoreType.DMA(()),
            pltpu.SemaphoreType.DMA((3, 2)),
            pltpu.SemaphoreType.DMA((3, 2)),
        ],
        compiler_params=pltpu.CompilerParams(collective_id=1, has_side_effects=True),
    )(acts, projector)


def per_device(acts, out_grad, projector, weight, first_moment, second_moment):
    assert lax.axis_size("tensor") == 4
    proj_hi = chip_gather(acts, projector)
    proj_hi = proj_hi.reshape(-1, proj_hi.shape[2])
    owners = lax.axis_size("dp")
    grad_blocks = out_grad.reshape(out_grad.shape[0], owners, -1)
    dims = (((0,), (0,)), ((), ()))
    partial = lax.dot_general(grad_blocks, proj_hi, dims, preferred_element_type=jnp.float32)
    blocks = lax.all_to_all(
        partial.astype(jnp.bfloat16), "dp", split_axis=0, concat_axis=0, tiled=True
    )
    new_weight, new_first, new_second = tail(
        blocks, first_moment[0], second_moment[0], projector, weight
    )
    return (new_weight, new_first[None], new_second[None])


def solution(mesh):
    return jax.shard_map(
        per_device,
        mesh=mesh,
        in_specs=(
            P(("dp", "tensor"), None),
            P("dp", "tensor"),
            P(),
            P("dp", "tensor"),
            P("tensor", "dp", None),
            P("tensor", "dp", None),
        ),
        out_specs=(P("dp", "tensor"), P("tensor", "dp", None), P("tensor", "dp", None)),
        check_vma=False,
    )
```

```python
import functools

import jax
import jax.numpy as jnp
from jax import lax
from jax.experimental import pallas as pl
from jax.experimental.pallas import tpu as pltpu
from jax.sharding import PartitionSpec as P

beta_first = 0.9
beta_second = 0.95
adam_step = 10
epsilon = 1e-08
step_rate = 0.5

MESH_ID = pl.DeviceIdType.MESH


def adam_moments(lowgrad, first_moment, second_moment):
    new_first = beta_first * first_moment + (1.0 - beta_first) * lowgrad
    new_second = beta_second * second_moment + (1.0 - beta_second) * lowgrad * lowgrad
    corrected_first = new_first / (1.0 - beta_first**adam_step)
    corrected_second = new_second / (1.0 - beta_second**adam_step)
    direction = (corrected_first / (jnp.sqrt(corrected_second) + epsilon)).astype(jnp.bfloat16)
    return (new_first, new_second, direction)


def tail_kernel(
    n, blocks_ref, first_ref, second_ref, proj_ref, weight_ref,
    new_weight_ref, new_first_ref, new_second_ref,
    blocks_v, direction_ref, update, sendbuf, recv, load_sem, local_sem, send_sem, recv_sem,
):
    me = lax.axis_index("dp")
    col = lax.axis_index("tensor")
    rows = sendbuf.shape[1]
    width = sendbuf.shape[2]
    barrier = pltpu.get_barrier_semaphore()
    for k in range(1, n):
        pl.semaphore_signal(
            barrier, inc=1, device_id=(lax.rem(me + k, n), col), device_id_type=MESH_ID
        )

    band = 16
    groups = 4
    span = blocks_v.shape[1] // groups
    loads = []
    for g in range(groups):
        rows_g = pl.ds(g * span, span)
        load = pltpu.make_async_copy(
            blocks_ref.at[:, rows_g, :], blocks_v.at[:, rows_g, :], load_sem.at[g]
        )
        load.start()
        loads.append(load)

    def rows_step(r, carry):
        rs = pl.ds(pl.multiple_of(r * band, band), band)
        lowgrad = blocks_v[0, rs, :].astype(jnp.float32)
        for k in range(1, n):
            lowgrad += blocks_v[k, rs, :].astype(jnp.float32)
        new_first, new_second, direction = adam_moments(
            lowgrad, first_ref[rs, :], second_ref[rs, :]
        )
        new_first_ref[rs, :] = new_first
        new_second_ref[rs, :] = new_second
        direction_ref[rs, :] = direction
        return carry

    for g in range(groups):
        loads[g].wait()
        lax.fori_loop(g * span // band, (g + 1) * span // band, rows_step, 0)

    update[...] = (
        lax.dot_general(
            proj_ref[...],
            direction_ref[...],
            (((1,), (1,)), ((), ())),
            preferred_element_type=jnp.float32,
        )
        .astype(jnp.bfloat16)
        .reshape(update.shape)
    )
    local = pltpu.make_async_copy(update, sendbuf, local_sem)
    local.start()
    local.wait()
    pl.semaphore_wait(barrier, n - 1)
    copies = []
    for k in range(1, n):
        dest = lax.rem(me + k, n)
        copy = pltpu.make_async_remote_copy(
            src_ref=sendbuf.at[dest],
            dst_ref=recv.at[k],
            send_sem=send_sem.at[k],
            recv_sem=recv_sem.at[k],
            device_id=(dest, col),
            device_id_type=MESH_ID,
        )
        copy.start()
        copies.append(copy)

    def apply(source, block):
        cols = pl.ds(pl.multiple_of(source * width, width), width)
        new_weight_ref[:, cols] = (
            weight_ref[:, cols].astype(jnp.float32) - step_rate * block.astype(jnp.float32)
        ).astype(jnp.bfloat16)

    apply(me, sendbuf[me])
    for k, copy in enumerate(copies, 1):
        copy.wait()
        apply(lax.rem(me + n - k, n), recv[k])


def tail(blocks, first_moment, second_moment, projector, weight):
    n, hidden, rank = blocks.shape
    rows = weight.shape[0]
    vmem = pl.BlockSpec(memory_space=pltpu.VMEM)
    return pl.pallas_call(
        functools.partial(tail_kernel, n),
        out_shape=(
            jax.ShapeDtypeStruct(weight.shape, weight.dtype),
            jax.ShapeDtypeStruct((hidden, rank), jnp.float32),
            jax.ShapeDtypeStruct((hidden, rank), jnp.float32),
        ),
        in_specs=[pl.BlockSpec(memory_space=pl.ANY)] + [vmem] * 4,
        out_specs=(vmem, vmem, vmem),
        scratch_shapes=[
            pltpu.VMEM(blocks.shape, blocks.dtype),
            pltpu.VMEM((hidden, rank), jnp.bfloat16),
            pltpu.VMEM((n, rows, hidden), jnp.bfloat16),
            pltpu.VMEM((n, rows, hidden), jnp.bfloat16),
            pltpu.VMEM((n, rows, hidden), jnp.bfloat16),
            pltpu.SemaphoreType.DMA((4,)),
            pltpu.SemaphoreType.DMA(()),
            pltpu.SemaphoreType.DMA((n,)),
            pltpu.SemaphoreType.DMA((n,)),
        ],
        compiler_params=pltpu.CompilerParams(
            collective_id=2, has_side_effects=True, vmem_limit_bytes=48 * 1024 * 1024
        ),
    )(blocks, first_moment, second_moment, projector, weight)


def chip_gather_kernel(
    acts_ref, proj_ref, hi_ref, q_buf, send_buf, recv, local_sem, send_sem, recv_sem
):
    me = lax.axis_index("tensor")
    core_peer = me + 1 - 2 * lax.rem(me, 2)
    chip_peer = lax.rem(me + 2, 4)
    barrier = pltpu.get_barrier_semaphore()
    for peer in (core_peer, chip_peer):
        pl.semaphore_signal(barrier, inc=1, device_id={"tensor": peer}, device_id_type=MESH_ID)
    q_buf[...] = jnp.dot(acts_ref[...], proj_ref[...], preferred_element_type=jnp.float32).astype(
        jnp.bfloat16
    )
    local = pltpu.make_async_copy(q_buf, send_buf, local_sem)
    local.start()
    local.wait()
    pl.semaphore_wait(barrier, 2)

    half = send_buf.shape[0] // 2

    def send(src, slot, peer, p):
        span = pl.ds(p * half, half)
        copy = pltpu.make_async_remote_copy(
            src_ref=src.at[span],
            dst_ref=recv.at[slot, span],
            send_sem=send_sem.at[slot, p],
            recv_sem=recv_sem.at[slot, p],
            device_id={"tensor": peer},
            device_id_type=MESH_ID,
        )
        copy.start()
        return copy

    def split(slot, piece):
        hi_ref[slot] = piece

    across = [send(send_buf, 1, chip_peer, p) for p in range(2)]
    beside = [send(send_buf, 0, core_peer, p) for p in range(2)]
    split(me, send_buf[...])
    forward = []
    for p in range(2):
        across[p].wait()
        forward.append(send(recv.at[1], 2, core_peer, p))
    split(chip_peer, recv[1])
    for copy in beside:
        copy.wait()
    split(core_peer, recv[0])
    for copy in forward:
        copy.wait()
    split(3 - me, recv[2])


def chip_gather(acts, projector):
    shape = (acts.shape[0], projector.shape[1])
    vmem = pl.BlockSpec(memory_space=pltpu.VMEM)
    return pl.pallas_call(
        chip_gather_kernel,
        out_shape=jax.ShapeDtypeStruct((4,) + shape, jnp.bfloat16),
        in_specs=[vmem, vmem],
        out_specs=vmem,
        scratch_shapes=[
            pltpu.VMEM(shape, jnp.bfloat16),
            pltpu.VMEM(shape, jnp.bfloat16),
            pltpu.VMEM((3,) + shape, jnp.bfloat16),
            pltpu.SemaphoreType.DMA(()),
            pltpu.SemaphoreType.DMA((3, 2)),
            pltpu.SemaphoreType.DMA((3, 2)),
        ],
        compiler_params=pltpu.CompilerParams(
            collective_id=1, has_side_effects=True, vmem_limit_bytes=48 * 1024 * 1024
        ),
    )(acts, projector)


def per_device(acts, out_grad, projector, weight, first_moment, second_moment):
    assert lax.axis_size("tensor") == 4
    proj_hi = chip_gather(acts, projector)
    proj_hi = proj_hi.reshape(-1, proj_hi.shape[2])
    owners = lax.axis_size("dp")
    grad_blocks = out_grad.reshape(out_grad.shape[0], owners, -1)
    dims = (((0,), (0,)), ((), ()))
    partial = lax.dot_general(grad_blocks, proj_hi, dims, preferred_element_type=jnp.float32)
    blocks = lax.all_to_all(
        partial.astype(jnp.bfloat16), "dp", split_axis=0, concat_axis=0, tiled=True
    )
    new_weight, new_first, new_second = tail(
        blocks, first_moment[0], second_moment[0], projector, weight
    )
    return (new_weight, new_first[None], new_second[None])


def solution(mesh):
    return jax.shard_map(
        per_device,
        mesh=mesh,
        in_specs=(
            P(("dp", "tensor"), None),
            P("dp", "tensor"),
            P(),
            P("dp", "tensor"),
            P("tensor", "dp", None),
            P("tensor", "dp", None),
        ),
        out_specs=(P("dp", "tensor"), P("tensor", "dp", None), P("tensor", "dp", None)),
        check_vma=False,
    )
```

```python
import functools

import jax
import jax.numpy as jnp
from jax import lax
from jax.experimental import pallas as pl
from jax.experimental.pallas import tpu as pltpu
from jax.sharding import PartitionSpec as P

beta_first = 0.9
beta_second = 0.95
adam_step = 10
epsilon = 1e-08
step_rate = 0.5

MESH_ID = pl.DeviceIdType.MESH


def adam_moments(lowgrad, first_moment, second_moment):
    new_first = beta_first * first_moment + (1.0 - beta_first) * lowgrad
    new_second = beta_second * second_moment + (1.0 - beta_second) * lowgrad * lowgrad
    corrected_first = new_first / (1.0 - beta_first**adam_step)
    corrected_second = new_second / (1.0 - beta_second**adam_step)
    direction = (corrected_first / (jnp.sqrt(corrected_second) + epsilon)).astype(jnp.bfloat16)
    return (new_first, new_second, direction)


def tail_kernel(
    n, blocks_ref, first_ref, second_ref, proj_ref, weight_ref,
    new_weight_ref, new_first_ref, new_second_ref,
    blocks_v, direction_ref, update, sendbuf, recv, load_sem, local_sem, send_sem, recv_sem,
):
    me = lax.axis_index("dp")
    col = lax.axis_index("tensor")
    rows = sendbuf.shape[1]
    width = sendbuf.shape[2]
    barrier = pltpu.get_barrier_semaphore()
    for k in range(1, n):
        pl.semaphore_signal(
            barrier, inc=1, device_id=(lax.rem(me + k, n), col), device_id_type=MESH_ID
        )

    band = 16
    groups = 4
    span = blocks_v.shape[1] // groups
    loads = []
    for g in range(groups):
        rows_g = pl.ds(g * span, span)
        load = pltpu.make_async_copy(
            blocks_ref.at[:, rows_g, :], blocks_v.at[:, rows_g, :], load_sem.at[g]
        )
        load.start()
        loads.append(load)

    def rows_step(r, carry):
        rs = pl.ds(pl.multiple_of(r * band, band), band)
        lowgrad = blocks_v[0, rs, :].astype(jnp.float32)
        for k in range(1, n):
            lowgrad += blocks_v[k, rs, :].astype(jnp.float32)
        new_first, new_second, direction = adam_moments(
            lowgrad, first_ref[rs, :], second_ref[rs, :]
        )
        new_first_ref[rs, :] = new_first
        new_second_ref[rs, :] = new_second
        direction_ref[rs, :] = direction
        return carry

    for g in range(groups):
        loads[g].wait()
        lax.fori_loop(g * span // band, (g + 1) * span // band, rows_step, 0)

    update[...] = (
        lax.dot_general(
            proj_ref[...],
            direction_ref[...],
            (((1,), (1,)), ((), ())),
            preferred_element_type=jnp.float32,
        )
        .astype(jnp.bfloat16)
        .reshape(update.shape)
    )
    local = pltpu.make_async_copy(update, sendbuf, local_sem)
    local.start()
    local.wait()
    pl.semaphore_wait(barrier, n - 1)
    copies = []
    for k in range(1, n):
        dest = lax.rem(me + k, n)
        copy = pltpu.make_async_remote_copy(
            src_ref=sendbuf.at[dest],
            dst_ref=recv.at[k],
            send_sem=send_sem.at[k],
            recv_sem=recv_sem.at[k],
            device_id=(dest, col),
            device_id_type=MESH_ID,
        )
        copy.start()
        copies.append(copy)

    def apply(source, block):
        cols = pl.ds(pl.multiple_of(source * width, width), width)
        new_weight_ref[:, cols] = (
            weight_ref[:, cols].astype(jnp.float32) - step_rate * block.astype(jnp.float32)
        ).astype(jnp.bfloat16)

    apply(me, sendbuf[me])
    for k, copy in enumerate(copies, 1):
        copy.wait()
        apply(lax.rem(me + n - k, n), recv[k])


def tail(blocks, first_moment, second_moment, projector, weight):
    n, hidden, rank = blocks.shape
    rows = weight.shape[0]
    vmem = pl.BlockSpec(memory_space=pltpu.VMEM)
    return pl.pallas_call(
        functools.partial(tail_kernel, n),
        out_shape=(
            jax.ShapeDtypeStruct(weight.shape, weight.dtype),
            jax.ShapeDtypeStruct((hidden, rank), jnp.float32),
            jax.ShapeDtypeStruct((hidden, rank), jnp.float32),
        ),
        in_specs=[pl.BlockSpec(memory_space=pl.ANY)] + [vmem] * 4,
        out_specs=(vmem, vmem, vmem),
        scratch_shapes=[
            pltpu.VMEM(blocks.shape, blocks.dtype),
            pltpu.VMEM((hidden, rank), jnp.bfloat16),
            pltpu.VMEM((n, rows, hidden), jnp.bfloat16),
            pltpu.VMEM((n, rows, hidden), jnp.bfloat16),
            pltpu.VMEM((n, rows, hidden), jnp.bfloat16),
            pltpu.SemaphoreType.DMA((4,)),
            pltpu.SemaphoreType.DMA(()),
            pltpu.SemaphoreType.DMA((n,)),
            pltpu.SemaphoreType.DMA((n,)),
        ],
        compiler_params=pltpu.CompilerParams(
            collective_id=2, has_side_effects=True, vmem_limit_bytes=48 * 1024 * 1024
        ),
    )(blocks, first_moment, second_moment, projector, weight)


def chip_gather_kernel(q_ref, hi_ref, recv, send_sem, recv_sem):
    me = lax.axis_index("tensor")
    core_peer = me + 1 - 2 * lax.rem(me, 2)
    chip_peer = lax.rem(me + 2, 4)
    barrier = pltpu.get_barrier_semaphore()
    for peer in (core_peer, chip_peer):
        pl.semaphore_signal(barrier, inc=1, device_id={"tensor": peer}, device_id_type=MESH_ID)
    send_buf = q_ref
    pl.semaphore_wait(barrier, 2)

    half = send_buf.shape[0] // 2

    def send(src, slot, peer, p):
        span = pl.ds(p * half, half)
        copy = pltpu.make_async_remote_copy(
            src_ref=src.at[span],
            dst_ref=recv.at[slot, span],
            send_sem=send_sem.at[slot, p],
            recv_sem=recv_sem.at[slot, p],
            device_id={"tensor": peer},
            device_id_type=MESH_ID,
        )
        copy.start()
        return copy

    def split(slot, piece):
        hi_ref[slot] = piece

    across = [send(send_buf, 1, chip_peer, p) for p in range(2)]
    beside = [send(send_buf, 0, core_peer, p) for p in range(2)]
    split(me, send_buf[...])
    forward = []
    for p in range(2):
        across[p].wait()
        forward.append(send(recv.at[1], 2, core_peer, p))
    split(chip_peer, recv[1])
    for copy in beside:
        copy.wait()
    split(core_peer, recv[0])
    for copy in forward:
        copy.wait()
    split(3 - me, recv[2])


def chip_gather(q):
    vmem = pl.BlockSpec(memory_space=pltpu.VMEM)
    return pl.pallas_call(
        chip_gather_kernel,
        out_shape=jax.ShapeDtypeStruct((4,) + q.shape, q.dtype),
        in_specs=[vmem],
        out_specs=vmem,
        scratch_shapes=[
            pltpu.VMEM((3,) + q.shape, q.dtype),
            pltpu.SemaphoreType.DMA((3, 2)),
            pltpu.SemaphoreType.DMA((3, 2)),
        ],
        compiler_params=pltpu.CompilerParams(collective_id=1, has_side_effects=True),
    )(q)


def per_device(acts, out_grad, projector, weight, first_moment, second_moment):
    assert lax.axis_size("tensor") == 4
    token_proj = jnp.dot(acts, projector, preferred_element_type=jnp.float32)
    proj_hi = chip_gather(token_proj.astype(jnp.bfloat16))
    proj_hi = proj_hi.reshape(-1, proj_hi.shape[2])
    owners = lax.axis_size("dp")
    grad_blocks = out_grad.reshape(out_grad.shape[0], owners, -1)
    dims = (((0,), (0,)), ((), ()))
    partial = lax.dot_general(grad_blocks, proj_hi, dims, preferred_element_type=jnp.float32)
    blocks = lax.all_to_all(
        partial.astype(jnp.bfloat16), "dp", split_axis=0, concat_axis=0, tiled=True
    )
    new_weight, new_first, new_second = tail(
        blocks, first_moment[0], second_moment[0], projector, weight
    )
    return (new_weight, new_first[None], new_second[None])


def solution(mesh):
    return jax.shard_map(
        per_device,
        mesh=mesh,
        in_specs=(
            P(("dp", "tensor"), None),
            P("dp", "tensor"),
            P(),
            P("dp", "tensor"),
            P("tensor", "dp", None),
            P("tensor", "dp", None),
        ),
        out_specs=(P("dp", "tensor"), P("tensor", "dp", None), P("tensor", "dp", None)),
        check_vma=False,
    )
```

```python
import functools

import jax
import jax.numpy as jnp
from jax import lax
from jax.experimental import pallas as pl
from jax.experimental.pallas import tpu as pltpu
from jax.sharding import PartitionSpec as P

beta_first = 0.9
beta_second = 0.95
adam_step = 10
epsilon = 1e-08
step_rate = 0.5

MESH_ID = pl.DeviceIdType.MESH


def adam_moments(lowgrad, first_moment, second_moment):
    new_first = beta_first * first_moment + (1.0 - beta_first) * lowgrad
    new_second = beta_second * second_moment + (1.0 - beta_second) * lowgrad * lowgrad
    corrected_first = new_first / (1.0 - beta_first**adam_step)
    corrected_second = new_second / (1.0 - beta_second**adam_step)
    direction = (corrected_first / (jnp.sqrt(corrected_second) + epsilon)).astype(jnp.bfloat16)
    return (new_first, new_second, direction)


def tail_kernel(
    n, blocks_ref, first_ref, second_ref, proj_ref, weight_ref,
    new_weight_ref, new_first_ref, new_second_ref,
    blocks_v, direction_ref, update, sendbuf, recv, load_sem, local_sem, send_sem, recv_sem,
):
    me = lax.axis_index("dp")
    col = lax.axis_index("tensor")
    rows = sendbuf.shape[1]
    width = sendbuf.shape[2]
    barrier = pltpu.get_barrier_semaphore()
    for k in range(1, n):
        pl.semaphore_signal(
            barrier, inc=1, device_id=(lax.rem(me + k, n), col), device_id_type=MESH_ID
        )

    band = 32
    groups = 8
    span = blocks_v.shape[1] // groups
    loads = []
    for g in range(groups):
        rows_g = pl.ds(g * span, span)
        load = pltpu.make_async_copy(
            blocks_ref.at[:, rows_g, :], blocks_v.at[:, rows_g, :], load_sem.at[g]
        )
        load.start()
        loads.append(load)

    def rows_step(r, carry):
        rs = pl.ds(pl.multiple_of(r * band, band), band)
        lowgrad = blocks_v[0, rs, :].astype(jnp.float32)
        for k in range(1, n):
            lowgrad += blocks_v[k, rs, :].astype(jnp.float32)
        new_first, new_second, direction = adam_moments(
            lowgrad, first_ref[rs, :], second_ref[rs, :]
        )
        new_first_ref[rs, :] = new_first
        new_second_ref[rs, :] = new_second
        direction_ref[rs, :] = direction
        return carry

    for g in range(groups):
        loads[g].wait()
        lax.fori_loop(g * span // band, (g + 1) * span // band, rows_step, 0)

    update[...] = (
        lax.dot_general(
            proj_ref[...],
            direction_ref[...],
            (((1,), (1,)), ((), ())),
            preferred_element_type=jnp.float32,
        )
        .astype(jnp.bfloat16)
        .reshape(update.shape)
    )
    local = pltpu.make_async_copy(update, sendbuf, local_sem)
    local.start()
    local.wait()
    pl.semaphore_wait(barrier, n - 1)
    copies = []
    for k in range(1, n):
        dest = lax.rem(me + k, n)
        copy = pltpu.make_async_remote_copy(
            src_ref=sendbuf.at[dest],
            dst_ref=recv.at[k],
            send_sem=send_sem.at[k],
            recv_sem=recv_sem.at[k],
            device_id=(dest, col),
            device_id_type=MESH_ID,
        )
        copy.start()
        copies.append(copy)

    def apply(source, block):
        cols = pl.ds(pl.multiple_of(source * width, width), width)
        new_weight_ref[:, cols] = (
            weight_ref[:, cols].astype(jnp.float32) - step_rate * block.astype(jnp.float32)
        ).astype(jnp.bfloat16)

    apply(me, sendbuf[me])
    for k, copy in enumerate(copies, 1):
        copy.wait()
        apply(lax.rem(me + n - k, n), recv[k])


def tail(blocks, first_moment, second_moment, projector, weight):
    n, hidden, rank = blocks.shape
    rows = weight.shape[0]
    vmem = pl.BlockSpec(memory_space=pltpu.VMEM)
    return pl.pallas_call(
        functools.partial(tail_kernel, n),
        out_shape=(
            jax.ShapeDtypeStruct(weight.shape, weight.dtype),
            jax.ShapeDtypeStruct((hidden, rank), jnp.float32),
            jax.ShapeDtypeStruct((hidden, rank), jnp.float32),
        ),
        in_specs=[pl.BlockSpec(memory_space=pl.ANY)] + [vmem] * 4,
        out_specs=(vmem, vmem, vmem),
        scratch_shapes=[
            pltpu.VMEM(blocks.shape, blocks.dtype),
            pltpu.VMEM((hidden, rank), jnp.bfloat16),
            pltpu.VMEM((n, rows, hidden), jnp.bfloat16),
            pltpu.VMEM((n, rows, hidden), jnp.bfloat16),
            pltpu.VMEM((n, rows, hidden), jnp.bfloat16),
            pltpu.SemaphoreType.DMA((8,)),
            pltpu.SemaphoreType.DMA(()),
            pltpu.SemaphoreType.DMA((n,)),
            pltpu.SemaphoreType.DMA((n,)),
        ],
        compiler_params=pltpu.CompilerParams(
            collective_id=2, has_side_effects=True, vmem_limit_bytes=48 * 1024 * 1024
        ),
    )(blocks, first_moment, second_moment, projector, weight)


def chip_gather_kernel(
    acts_ref, proj_ref, hi_ref, q_buf, send_buf, recv, local_sem, send_sem, recv_sem
):
    me = lax.axis_index("tensor")
    core_peer = me + 1 - 2 * lax.rem(me, 2)
    chip_peer = lax.rem(me + 2, 4)
    barrier = pltpu.get_barrier_semaphore()
    for peer in (core_peer, chip_peer):
        pl.semaphore_signal(barrier, inc=1, device_id={"tensor": peer}, device_id_type=MESH_ID)
    q_buf[...] = jnp.dot(acts_ref[...], proj_ref[...], preferred_element_type=jnp.float32).astype(
        jnp.bfloat16
    )
    local = pltpu.make_async_copy(q_buf, send_buf, local_sem)
    local.start()
    local.wait()
    pl.semaphore_wait(barrier, 2)

    def send(src, slot, peer):
        copy = pltpu.make_async_remote_copy(
            src_ref=src,
            dst_ref=recv.at[slot],
            send_sem=send_sem.at[slot],
            recv_sem=recv_sem.at[slot],
            device_id={"tensor": peer},
            device_id_type=MESH_ID,
        )
        copy.start()
        return copy

    def split(slot, piece):
        hi_ref[slot] = piece

    across = send(send_buf, 1, chip_peer)
    beside = send(send_buf, 0, core_peer)
    split(me, send_buf[...])
    across.wait()
    forward = send(recv.at[1], 2, core_peer)
    split(chip_peer, recv[1])
    beside.wait()
    split(core_peer, recv[0])
    forward.wait()
    split(3 - me, recv[2])


def chip_gather(acts, projector):
    shape = (acts.shape[0], projector.shape[1])
    vmem = pl.BlockSpec(memory_space=pltpu.VMEM)
    return pl.pallas_call(
        chip_gather_kernel,
        out_shape=jax.ShapeDtypeStruct((4,) + shape, jnp.bfloat16),
        in_specs=[vmem, vmem],
        out_specs=vmem,
        scratch_shapes=[
            pltpu.VMEM(shape, jnp.bfloat16),
            pltpu.VMEM(shape, jnp.bfloat16),
            pltpu.VMEM((3,) + shape, jnp.bfloat16),
            pltpu.SemaphoreType.DMA(()),
            pltpu.SemaphoreType.DMA((3,)),
            pltpu.SemaphoreType.DMA((3,)),
        ],
        compiler_params=pltpu.CompilerParams(
            collective_id=1, has_side_effects=True, vmem_limit_bytes=48 * 1024 * 1024
        ),
    )(acts, projector)


def per_device(acts, out_grad, projector, weight, first_moment, second_moment):
    assert lax.axis_size("tensor") == 4
    proj_hi = chip_gather(acts, projector)
    proj_hi = proj_hi.reshape(-1, proj_hi.shape[2])
    owners = lax.axis_size("dp")
    grad_blocks = out_grad.reshape(out_grad.shape[0], owners, -1)
    dims = (((0,), (0,)), ((), ()))
    partial = lax.dot_general(grad_blocks, proj_hi, dims, preferred_element_type=jnp.float32)
    blocks = lax.all_to_all(
        partial.astype(jnp.bfloat16), "dp", split_axis=0, concat_axis=0, tiled=True
    )
    new_weight, new_first, new_second = tail(
        blocks, first_moment[0], second_moment[0], projector, weight
    )
    return (new_weight, new_first[None], new_second[None])


def solution(mesh):
    return jax.shard_map(
        per_device,
        mesh=mesh,
        in_specs=(
            P(("dp", "tensor"), None),
            P("dp", "tensor"),
            P(),
            P("dp", "tensor"),
            P("tensor", "dp", None),
            P("tensor", "dp", None),
        ),
        out_specs=(P("dp", "tensor"), P("tensor", "dp", None), P("tensor", "dp", None)),
        check_vma=False,
    )
```

```python
import functools

import jax
import jax.numpy as jnp
from jax import lax
from jax.experimental import pallas as pl
from jax.experimental.pallas import tpu as pltpu
from jax.sharding import PartitionSpec as P

beta_first = 0.9
beta_second = 0.95
adam_step = 10
epsilon = 1e-08
step_rate = 0.5

MESH_ID = pl.DeviceIdType.MESH


def adam_moments(lowgrad, first_moment, second_moment):
    new_first = beta_first * first_moment + (1.0 - beta_first) * lowgrad
    new_second = beta_second * second_moment + (1.0 - beta_second) * lowgrad * lowgrad
    corrected_first = new_first / (1.0 - beta_first**adam_step)
    corrected_second = new_second / (1.0 - beta_second**adam_step)
    direction = (corrected_first / (jnp.sqrt(corrected_second) + epsilon)).astype(jnp.bfloat16)
    return (new_first, new_second, direction)


def tail_kernel(
    n, blocks_ref, first_ref, second_ref, proj_ref, weight_ref,
    new_weight_ref, new_first_ref, new_second_ref,
    blocks_v, direction_ref, update, sendbuf, recv, load_sem, local_sem, send_sem, recv_sem,
):
    me = lax.axis_index("dp")
    col = lax.axis_index("tensor")
    rows = sendbuf.shape[1]
    width = sendbuf.shape[2]
    barrier = pltpu.get_barrier_semaphore()
    for k in range(1, n):
        pl.semaphore_signal(
            barrier, inc=1, device_id=(lax.rem(me + k, n), col), device_id_type=MESH_ID
        )

    band = 16
    groups = 4
    span = blocks_v.shape[1] // groups
    loads = []
    for g in range(groups):
        rows_g = pl.ds(g * span, span)
        load = pltpu.make_async_copy(
            blocks_ref.at[:, rows_g, :], blocks_v.at[:, rows_g, :], load_sem.at[g]
        )
        load.start()
        loads.append(load)

    def rows_step(r, carry):
        rs = pl.ds(pl.multiple_of(r * band, band), band)
        lowgrad = blocks_v[0, rs, :].astype(jnp.float32)
        for k in range(1, n):
            lowgrad += blocks_v[k, rs, :].astype(jnp.float32)
        new_first, new_second, direction = adam_moments(
            lowgrad, first_ref[rs, :], second_ref[rs, :]
        )
        new_first_ref[rs, :] = new_first
        new_second_ref[rs, :] = new_second
        direction_ref[rs, :] = direction
        return carry

    for g in range(groups):
        loads[g].wait()
        lax.fori_loop(g * span // band, (g + 1) * span // band, rows_step, 0)

    update[...] = (
        lax.dot_general(
            proj_ref[...],
            direction_ref[...],
            (((1,), (1,)), ((), ())),
            preferred_element_type=jnp.float32,
        )
        .astype(jnp.bfloat16)
        .reshape(update.shape)
    )
    pl.semaphore_wait(barrier, n - 1)
    locals_ = []
    for k in range(n):
        dest = lax.rem(me + k, n)
        local = pltpu.make_async_copy(update.at[dest], sendbuf.at[dest], local_sem.at[k])
        local.start()
        locals_.append(local)
    copies = []
    for k in range(1, n):
        dest = lax.rem(me + k, n)
        locals_[k].wait()
        copy = pltpu.make_async_remote_copy(
            src_ref=sendbuf.at[dest],
            dst_ref=recv.at[k],
            send_sem=send_sem.at[k],
            recv_sem=recv_sem.at[k],
            device_id=(dest, col),
            device_id_type=MESH_ID,
        )
        copy.start()
        copies.append(copy)
    locals_[0].wait()

    def apply(source, block):
        cols = pl.ds(pl.multiple_of(source * width, width), width)
        new_weight_ref[:, cols] = (
            weight_ref[:, cols].astype(jnp.float32) - step_rate * block.astype(jnp.float32)
        ).astype(jnp.bfloat16)

    apply(me, sendbuf[me])
    for k, copy in enumerate(copies, 1):
        copy.wait()
        apply(lax.rem(me + n - k, n), recv[k])


def tail(blocks, first_moment, second_moment, projector, weight):
    n, hidden, rank = blocks.shape
    rows = weight.shape[0]
    vmem = pl.BlockSpec(memory_space=pltpu.VMEM)
    return pl.pallas_call(
        functools.partial(tail_kernel, n),
        out_shape=(
            jax.ShapeDtypeStruct(weight.shape, weight.dtype),
            jax.ShapeDtypeStruct((hidden, rank), jnp.float32),
            jax.ShapeDtypeStruct((hidden, rank), jnp.float32),
        ),
        in_specs=[pl.BlockSpec(memory_space=pl.ANY)] + [vmem] * 4,
        out_specs=(vmem, vmem, vmem),
        scratch_shapes=[
            pltpu.VMEM(blocks.shape, blocks.dtype),
            pltpu.VMEM((hidden, rank), jnp.bfloat16),
            pltpu.VMEM((n, rows, hidden), jnp.bfloat16),
            pltpu.VMEM((n, rows, hidden), jnp.bfloat16),
            pltpu.VMEM((n, rows, hidden), jnp.bfloat16),
            pltpu.SemaphoreType.DMA((4,)),
            pltpu.SemaphoreType.DMA((n,)),
            pltpu.SemaphoreType.DMA((n,)),
            pltpu.SemaphoreType.DMA((n,)),
        ],
        compiler_params=pltpu.CompilerParams(
            collective_id=2, has_side_effects=True, vmem_limit_bytes=48 * 1024 * 1024
        ),
    )(blocks, first_moment, second_moment, projector, weight)


def chip_gather_kernel(
    acts_ref, proj_ref, hi_ref, q_buf, send_buf, recv, local_sem, send_sem, recv_sem
):
    me = lax.axis_index("tensor")
    core_peer = me + 1 - 2 * lax.rem(me, 2)
    chip_peer = lax.rem(me + 2, 4)
    barrier = pltpu.get_barrier_semaphore()
    for peer in (core_peer, chip_peer):
        pl.semaphore_signal(barrier, inc=1, device_id={"tensor": peer}, device_id_type=MESH_ID)
    q_buf[...] = jnp.dot(acts_ref[...], proj_ref[...], preferred_element_type=jnp.float32).astype(
        jnp.bfloat16
    )
    local = pltpu.make_async_copy(q_buf, send_buf, local_sem)
    local.start()
    local.wait()
    pl.semaphore_wait(barrier, 2)

    half = send_buf.shape[0] // 2

    def send(src, slot, peer, p):
        span = pl.ds(p * half, half)
        copy = pltpu.make_async_remote_copy(
            src_ref=src.at[span],
            dst_ref=recv.at[slot, span],
            send_sem=send_sem.at[slot, p],
            recv_sem=recv_sem.at[slot, p],
            device_id={"tensor": peer},
            device_id_type=MESH_ID,
        )
        copy.start()
        return copy

    def split(slot, piece):
        hi_ref[slot] = piece

    across = [send(send_buf, 1, chip_peer, p) for p in range(2)]
    beside = [send(send_buf, 0, core_peer, p) for p in range(2)]
    split(me, send_buf[...])
    forward = []
    for p in range(2):
        across[p].wait()
        forward.append(send(recv.at[1], 2, core_peer, p))
    split(chip_peer, recv[1])
    for copy in beside:
        copy.wait()
    split(core_peer, recv[0])
    for copy in forward:
        copy.wait()
    split(3 - me, recv[2])


def chip_gather(acts, projector):
    shape = (acts.shape[0], projector.shape[1])
    vmem = pl.BlockSpec(memory_space=pltpu.VMEM)
    return pl.pallas_call(
        chip_gather_kernel,
        out_shape=jax.ShapeDtypeStruct((4,) + shape, jnp.bfloat16),
        in_specs=[vmem, vmem],
        out_specs=vmem,
        scratch_shapes=[
            pltpu.VMEM(shape, jnp.bfloat16),
            pltpu.VMEM(shape, jnp.bfloat16),
            pltpu.VMEM((3,) + shape, jnp.bfloat16),
            pltpu.SemaphoreType.DMA(()),
            pltpu.SemaphoreType.DMA((3, 2)),
            pltpu.SemaphoreType.DMA((3, 2)),
        ],
        compiler_params=pltpu.CompilerParams(
            collective_id=1, has_side_effects=True, vmem_limit_bytes=48 * 1024 * 1024
        ),
    )(acts, projector)


def per_device(acts, out_grad, projector, weight, first_moment, second_moment):
    assert lax.axis_size("tensor") == 4
    proj_hi = chip_gather(acts, projector)
    proj_hi = proj_hi.reshape(-1, proj_hi.shape[2])
    owners = lax.axis_size("dp")
    grad_blocks = out_grad.reshape(out_grad.shape[0], owners, -1)
    dims = (((0,), (0,)), ((), ()))
    partial = lax.dot_general(grad_blocks, proj_hi, dims, preferred_element_type=jnp.float32)
    blocks = lax.all_to_all(
        partial.astype(jnp.bfloat16), "dp", split_axis=0, concat_axis=0, tiled=True
    )
    new_weight, new_first, new_second = tail(
        blocks, first_moment[0], second_moment[0], projector, weight
    )
    return (new_weight, new_first[None], new_second[None])


def solution(mesh):
    return jax.shard_map(
        per_device,
        mesh=mesh,
        in_specs=(
            P(("dp", "tensor"), None),
            P("dp", "tensor"),
            P(),
            P("dp", "tensor"),
            P("tensor", "dp", None),
            P("tensor", "dp", None),
        ),
        out_specs=(P("dp", "tensor"), P("tensor", "dp", None), P("tensor", "dp", None)),
        check_vma=False,
    )
```

```python
import functools

import jax
import jax.numpy as jnp
from jax import lax
from jax.experimental import pallas as pl
from jax.experimental.pallas import tpu as pltpu
from jax.sharding import PartitionSpec as P

beta_first = 0.9
beta_second = 0.95
adam_step = 10
epsilon = 1e-08
step_rate = 0.5

MESH_ID = pl.DeviceIdType.MESH


def adam_moments(lowgrad, first_moment, second_moment):
    new_first = beta_first * first_moment + (1.0 - beta_first) * lowgrad
    new_second = beta_second * second_moment + (1.0 - beta_second) * lowgrad * lowgrad
    corrected_first = new_first / (1.0 - beta_first**adam_step)
    corrected_second = new_second / (1.0 - beta_second**adam_step)
    direction = (corrected_first / (jnp.sqrt(corrected_second) + epsilon)).astype(jnp.bfloat16)
    return (new_first, new_second, direction)


def tail_kernel(
    n, blocks_ref, first_ref, second_ref, proj_ref, weight_ref,
    new_weight_ref, new_first_ref, new_second_ref,
    blocks_v, total, direction_ref, update, sendbuf, recv, load_sem, local_sem, send_sem, recv_sem,
):
    me = lax.axis_index("dp")
    col = lax.axis_index("tensor")
    rows = sendbuf.shape[1]
    width = sendbuf.shape[2]
    barrier = pltpu.get_barrier_semaphore()
    for k in range(1, n):
        pl.semaphore_signal(
            barrier, inc=1, device_id=(lax.rem(me + k, n), col), device_id_type=MESH_ID
        )

    band = 16
    groups = 4
    per = n // groups
    loads = []
    for g in range(groups):
        load = pltpu.make_async_copy(
            blocks_ref.at[pl.ds(g * per, per)], blocks_v.at[pl.ds(g * per, per)], load_sem.at[g]
        )
        load.start()
        loads.append(load)

    def group_step(g, last):
        def rows_step(r, carry):
            rs = pl.ds(pl.multiple_of(r * band, band), band)
            lowgrad = blocks_v[g * per, rs, :].astype(jnp.float32)
            for k in range(g * per + 1, (g + 1) * per):
                lowgrad += blocks_v[k, rs, :].astype(jnp.float32)
            if g > 0:
                lowgrad += total[rs, :]
            if not last:
                total[rs, :] = lowgrad
                return carry
            new_first, new_second, direction = adam_moments(
                lowgrad, first_ref[rs, :], second_ref[rs, :]
            )
            new_first_ref[rs, :] = new_first
            new_second_ref[rs, :] = new_second
            direction_ref[rs, :] = direction
            return carry

        lax.fori_loop(0, blocks_v.shape[1] // band, rows_step, 0)

    for g in range(groups):
        loads[g].wait()
        group_step(g, g == groups - 1)

    update[...] = (
        lax.dot_general(
            proj_ref[...],
            direction_ref[...],
            (((1,), (1,)), ((), ())),
            preferred_element_type=jnp.float32,
        )
        .astype(jnp.bfloat16)
        .reshape(update.shape)
    )
    local = pltpu.make_async_copy(update, sendbuf, local_sem)
    local.start()
    local.wait()
    pl.semaphore_wait(barrier, n - 1)
    copies = []
    for k in range(1, n):
        dest = lax.rem(me + k, n)
        copy = pltpu.make_async_remote_copy(
            src_ref=sendbuf.at[dest],
            dst_ref=recv.at[k],
            send_sem=send_sem.at[k],
            recv_sem=recv_sem.at[k],
            device_id=(dest, col),
            device_id_type=MESH_ID,
        )
        copy.start()
        copies.append(copy)

    def apply(source, block):
        cols = pl.ds(pl.multiple_of(source * width, width), width)
        new_weight_ref[:, cols] = (
            weight_ref[:, cols].astype(jnp.float32) - step_rate * block.astype(jnp.float32)
        ).astype(jnp.bfloat16)

    apply(me, sendbuf[me])
    for k, copy in enumerate(copies, 1):
        copy.wait()
        apply(lax.rem(me + n - k, n), recv[k])


def tail(blocks, first_moment, second_moment, projector, weight):
    n, hidden, rank = blocks.shape
    rows = weight.shape[0]
    vmem = pl.BlockSpec(memory_space=pltpu.VMEM)
    return pl.pallas_call(
        functools.partial(tail_kernel, n),
        out_shape=(
            jax.ShapeDtypeStruct(weight.shape, weight.dtype),
            jax.ShapeDtypeStruct((hidden, rank), jnp.float32),
            jax.ShapeDtypeStruct((hidden, rank), jnp.float32),
        ),
        in_specs=[pl.BlockSpec(memory_space=pl.ANY)] + [vmem] * 4,
        out_specs=(vmem, vmem, vmem),
        scratch_shapes=[
            pltpu.VMEM(blocks.shape, blocks.dtype),
            pltpu.VMEM((hidden, rank), jnp.float32),
            pltpu.VMEM((hidden, rank), jnp.bfloat16),
            pltpu.VMEM((n, rows, hidden), jnp.bfloat16),
            pltpu.VMEM((n, rows, hidden), jnp.bfloat16),
            pltpu.VMEM((n, rows, hidden), jnp.bfloat16),
            pltpu.SemaphoreType.DMA((4,)),
            pltpu.SemaphoreType.DMA(()),
            pltpu.SemaphoreType.DMA((n,)),
            pltpu.SemaphoreType.DMA((n,)),
        ],
        compiler_params=pltpu.CompilerParams(
            collective_id=2, has_side_effects=True, vmem_limit_bytes=48 * 1024 * 1024
        ),
    )(blocks, first_moment, second_moment, projector, weight)


def chip_gather_kernel(
    acts_ref, proj_ref, hi_ref, q_buf, send_buf, recv, local_sem, send_sem, recv_sem
):
    me = lax.axis_index("tensor")
    core_peer = me + 1 - 2 * lax.rem(me, 2)
    chip_peer = lax.rem(me + 2, 4)
    barrier = pltpu.get_barrier_semaphore()
    for peer in (core_peer, chip_peer):
        pl.semaphore_signal(barrier, inc=1, device_id={"tensor": peer}, device_id_type=MESH_ID)
    q_buf[...] = jnp.dot(acts_ref[...], proj_ref[...], preferred_element_type=jnp.float32).astype(
        jnp.bfloat16
    )
    local = pltpu.make_async_copy(q_buf, send_buf, local_sem)
    local.start()
    local.wait()
    pl.semaphore_wait(barrier, 2)

    half = send_buf.shape[0] // 2

    def send(src, slot, peer, p):
        span = pl.ds(p * half, half)
        copy = pltpu.make_async_remote_copy(
            src_ref=src.at[span],
            dst_ref=recv.at[slot, span],
            send_sem=send_sem.at[slot, p],
            recv_sem=recv_sem.at[slot, p],
            device_id={"tensor": peer},
            device_id_type=MESH_ID,
        )
        copy.start()
        return copy

    def split(slot, piece):
        hi_ref[slot] = piece

    across = [send(send_buf, 1, chip_peer, p) for p in range(2)]
    beside = [send(send_buf, 0, core_peer, p) for p in range(2)]
    split(me, send_buf[...])
    forward = []
    for p in range(2):
        across[p].wait()
        forward.append(send(recv.at[1], 2, core_peer, p))
    split(chip_peer, recv[1])
    for copy in beside:
        copy.wait()
    split(core_peer, recv[0])
    for copy in forward:
        copy.wait()
    split(3 - me, recv[2])


def chip_gather(acts, projector):
    shape = (acts.shape[0], projector.shape[1])
    vmem = pl.BlockSpec(memory_space=pltpu.VMEM)
    return pl.pallas_call(
        chip_gather_kernel,
        out_shape=jax.ShapeDtypeStruct((4,) + shape, jnp.bfloat16),
        in_specs=[vmem, vmem],
        out_specs=vmem,
        scratch_shapes=[
            pltpu.VMEM(shape, jnp.bfloat16),
            pltpu.VMEM(shape, jnp.bfloat16),
            pltpu.VMEM((3,) + shape, jnp.bfloat16),
            pltpu.SemaphoreType.DMA(()),
            pltpu.SemaphoreType.DMA((3, 2)),
            pltpu.SemaphoreType.DMA((3, 2)),
        ],
        compiler_params=pltpu.CompilerParams(
            collective_id=1, has_side_effects=True, vmem_limit_bytes=48 * 1024 * 1024
        ),
    )(acts, projector)


def per_device(acts, out_grad, projector, weight, first_moment, second_moment):
    assert lax.axis_size("tensor") == 4
    proj_hi = chip_gather(acts, projector)
    proj_hi = proj_hi.reshape(-1, proj_hi.shape[2])
    owners = lax.axis_size("dp")
    grad_blocks = out_grad.reshape(out_grad.shape[0], owners, -1)
    dims = (((0,), (0,)), ((), ()))
    partial = lax.dot_general(grad_blocks, proj_hi, dims, preferred_element_type=jnp.float32)
    blocks = lax.all_to_all(
        partial.astype(jnp.bfloat16), "dp", split_axis=0, concat_axis=0, tiled=True
    )
    new_weight, new_first, new_second = tail(
        blocks, first_moment[0], second_moment[0], projector, weight
    )
    return (new_weight, new_first[None], new_second[None])


def solution(mesh):
    return jax.shard_map(
        per_device,
        mesh=mesh,
        in_specs=(
            P(("dp", "tensor"), None),
            P("dp", "tensor"),
            P(),
            P("dp", "tensor"),
            P("tensor", "dp", None),
            P("tensor", "dp", None),
        ),
        out_specs=(P("dp", "tensor"), P("tensor", "dp", None), P("tensor", "dp", None)),
        check_vma=False,
    )
```
